256 devices in a mesh: dp: 8 (over z_hi, x), expert: 32 (over y, z_lo, core).
Axes of the slice: x: 4, y: 4, z: 8 (z_hi: 2, z_lo: 4; z = z_hi * 4 + z_lo), core: 2. Of those that a mesh axis runs over, the one named last changes fastest.
Arguments:
- tokens: bfloat16 [40960, 2048], P(('dp', 'expert')), may hold values from -6 to 6
- out_grad: bfloat16 [40960, 2048], P(('dp', 'expert')), may hold values from -6 to 6
- expert_ids: int32 [40960, 8], P(('dp', 'expert')), may hold values from 0 to 127, all different within a row; in each aligned block of 160 rows (0 to 159, 160 to 319, ...) at most 15 rows name the same one
- gate_vals: bfloat16 [40960, 8], P(('dp', 'expert')), may hold values from 0.049804688 to 0.59765625
- w_gate: bfloat16 [32, 2048, 768], P('expert'), may hold values from -0.125 to 0.125
- w_up: bfloat16 [32, 2048, 768], P('expert'), may hold values from -0.125 to 0.125
- w_down: bfloat16 [32, 768, 2048], P('expert'), may hold values from -0.21875 to 0.21875
Outputs:
- d_tokens: bfloat16 [40960, 2048], P(('dp', 'expert'))
- d_gates: bfloat16 [40960, 8], P(('dp', 'expert'))
- d_w_gate: bfloat16 [32, 2048, 768], P('expert', 'dp')
- d_w_up: bfloat16 [32, 2048, 768], P('expert', 'dp')
- d_w_down: bfloat16 [32, 768, 2048], P('expert', None, 'dp')
The draws below stay inside these ranges and needn't reach their ends.
Inputs may be any that keep to these rules, and one draw needn't show every extreme that they name: `expert_ids`: each row names 8 different experts and every expert is named somewhere. Among the 160 rows of one device no expert is named more than 15 times, a bound that some block reaches. Experts 32 and above lie outside this window.
All inputs are finite; a program needn't handle non-finite values.
Results may differ from the reference program's by a relative error of at most 0.012.
Values may be sent and summed in bfloat16 or wider, within the bound.
A program may use at most 128 MiB of HBM per device.

```python
import math
import jax
import jax.numpy as jnp
import numpy as np
from jax import lax

D = 2048
FF = 768
EXPERTS_ALL = 128
TOPK = 8
EXP_DEV = 1
TOK_DEV = 160
CAP = 15
EXPERTS = 32
TOKENS = 40960
N_DP = 8
N_EXPERT = 32


def levels(rng, dims, shards, smallest, high):
    def one(dim, shards_of):
        heights = jax.random.uniform(jax.random.fold_in(jax.random.fold_in(rng, 6), dim), (shards_of,), jnp.float32, smallest / len(shards), high / len(shards))
        return jnp.repeat(jnp.exp(heights), dims[dim] // shards_of).reshape((-1,) + (1,) * (len(dims) - dim - 1))

    gain = one(*shards[0])
    for cut in shards[1:]:
        gain = gain * one(*cut)
    return gain


def routed_block(stream_key, own, number, rows, number_of, top, limit, lean):
    ranking = jax.random.permutation(stream_key, number_of)
    packed, usual = portions_of(number_of, rows * top, limit, lean, True), portions_of(number_of, rows * top, limit, lean, False)
    places = jnp.arange(number_of)

    def named(sizes, turn):
        used = int((sizes > 0).sum())
        fixed = max(1, used // 4)
        passed = fixed + (places - fixed + turn * (used - fixed)) % max(1, number_of - fixed)
        return jnp.zeros((number_of,), jnp.int32).at[ranking[jnp.where(places < fixed, places, passed)]].set(jnp.asarray(sizes, jnp.int32))

    sizes = jnp.where(number % 4 == 0, named(packed, number // 4), named(usual, number - number // 4 - 1))
    mixed = jax.random.permutation(jax.random.fold_in(own, 3), number_of)
    donor, sink = mixed[0:number_of // 2 * 2:2], mixed[1:number_of // 2 * 2:2]
    room = jnp.minimum(sizes[donor] - 1, limit - sizes[sink]) // 2
    room = jnp.where((donor == ranking[0]) | (sink == ranking[0]) | (sizes[sink] == 0), 0, jnp.maximum(room, 0))
    passed = jax.random.randint(jax.random.fold_in(own, 4), (number_of // 2,), 0, 1 << 20) % (room + 1)
    sizes = sizes.at[donor].add(-passed).at[sink].add(passed)
    members = jnp.searchsorted(jnp.cumsum(sizes), jnp.arange(rows * top), side="right").astype(jnp.int32)
    grid = members.reshape(top, rows).T
    grid = grid[jax.random.permutation(jax.random.fold_in(own, 1), rows)]
    turn = jax.random.randint(jax.random.fold_in(own, 2), (rows, 1), 0, top)
    return jnp.take_along_axis(grid, (jnp.arange(top)[None, :] + turn) % top, axis=1)


def portions_of(count, total, bound, lean, full):
    loads = [(1 << 20) // math.isqrt(rank ** lean) + 1 for rank in range(1, count + 1)]
    largest = bound if full else min(bound, max(-(-total // count), total * loads[0] // sum(loads)))
    least = 1 if total - largest >= count - 1 else 0
    holding, rest = [largest] + [least] * (count - 1), total - largest - least * (count - 1)
    while rest > 0:
        candidates = [i for i in range(1, count) if holding[i] < largest] or [i for i in range(1, count) if holding[i] < bound]
        pool, remaining = sum([loads[i] for i in candidates]), rest
        for i in candidates:
            addition = min(bound - holding[i], max(1, remaining * loads[i] // pool), rest)
            holding[i] = holding[i] + addition
            rest = rest - addition
    return np.array(holding)


def bell_draw(stream_key, extent, spread, reach, split=(), kind=jnp.bfloat16):
    factor_of = levels(stream_key, extent, split, -0.22, 0.18) if split else 1.0
    array = jax.random.normal(stream_key, extent, jnp.float32) * spread * factor_of
    return jnp.minimum(jnp.maximum(array, -reach), reach).astype(kind)


def setup_inputs(seed: int = 0) -> dict:
    arg_keys = jax.random.split(jax.random.key(seed), 8)
    tokens = bell_draw(arg_keys[0], (TOKENS, D), 1.0, 6.0, ((0, 256),))
    out_grad = bell_draw(arg_keys[1], (TOKENS, D), 1.0, 6.0, ((0, 256),))
    expert_ids_keys = jax.random.split(jax.random.fold_in(arg_keys[2], 1), TOKENS // TOK_DEV)
    expert_ids_turns = jax.random.permutation(jax.random.fold_in(arg_keys[2], 3), TOKENS // TOK_DEV)
    expert_ids = jax.vmap(lambda own, number: routed_block(jax.random.fold_in(arg_keys[2], 2), own, number, TOK_DEV, EXPERTS_ALL, TOPK, CAP, 2))(expert_ids_keys, expert_ids_turns).reshape((TOKENS, TOPK))
    gate_vals = jnp.clip(jnp.exp(math.log(0.59765625) - 2.4849066 * jax.random.uniform(arg_keys[3], (TOKENS, TOPK), jnp.float32) ** levels(arg_keys[3], (TOKENS, TOPK), ((0, 256),), -0.2, 0.2)), 0.049804688, 0.59765625).astype(jnp.bfloat16)
    w_gate = bell_draw(arg_keys[4], (EXPERTS, D, FF), D ** -0.5, 0.125, ((0, 32),))
    w_up = bell_draw(arg_keys[5], (EXPERTS, D, FF), D ** -0.5, 0.125, ((0, 32),))
    w_down = bell_draw(arg_keys[6], (EXPERTS, FF, D), FF ** -0.5, 0.21875, ((0, 32),))
    return {"tokens": tokens, "out_grad": out_grad, "expert_ids": expert_ids, "gate_vals": gate_vals, "w_gate": w_gate, "w_up": w_up, "w_down": w_down}


def expert_rows(rows_x, rows_dy, rows_gate, gate_w, up_w, down_w):
    gate_pre = jnp.dot(rows_x, gate_w, preferred_element_type=jnp.float32)
    up_pre = jnp.dot(rows_x, up_w, preferred_element_type=jnp.float32)
    sigmoid_gate = jax.nn.sigmoid(gate_pre)
    silu_gate = gate_pre * sigmoid_gate
    hidden = (silu_gate * up_pre).astype(jnp.bfloat16)
    hidden_raw = lax.dot_general(rows_dy, down_w, (((1,), (1,)), ((), ())), preferred_element_type=jnp.float32)
    gate_scale = rows_gate.astype(jnp.float32)[:, None]
    gate_grad = jnp.sum(hidden.astype(jnp.float32) * hidden_raw, axis=1).astype(jnp.bfloat16)
    hidden_grad = gate_scale * hidden_raw
    up_grad = (hidden_grad * silu_gate).astype(jnp.bfloat16)
    pre_grad = (hidden_grad * up_pre * sigmoid_gate * (1.0 + gate_pre * (1.0 - sigmoid_gate))).astype(jnp.bfloat16)
    scaled_dy = (gate_scale * rows_dy.astype(jnp.float32)).astype(jnp.bfloat16)
    input_rows = lax.dot_general(pre_grad, gate_w, (((1,), (1,)), ((), ())), preferred_element_type=jnp.float32)
    input_rows = input_rows + lax.dot_general(up_grad, up_w, (((1,), (1,)), ((), ())), preferred_element_type=jnp.float32)
    return input_rows.astype(jnp.bfloat16), gate_grad, pre_grad, up_grad, hidden, scaled_dy


def reference(tokens, out_grad, expert_ids, gate_vals, w_gate, w_up, w_down):
    experts = EXP_DEV * N_EXPERT
    group_rows = N_EXPERT * TOK_DEV
    most_rows = N_EXPERT * CAP
    group_x = tokens.reshape(N_DP, group_rows, D)
    group_dy = out_grad.reshape(N_DP, group_rows, D)
    group_ids = expert_ids.reshape(N_DP, group_rows * TOPK)
    group_gates = gate_vals.reshape(N_DP, group_rows * TOPK)
    positions = jnp.arange(most_rows, dtype=jnp.int32)

    def one_expert(carried, expert):
        input_acc, gates_acc = carried
        gate_w = w_gate[expert]
        up_w = w_up[expert]
        down_w = w_down[expert]

        def one_member(totals, member):
            ids_m, x_m, dy_m, gates_m, in_acc, g_acc = member
            matched = ids_m == expert
            ordering = jnp.argsort(jnp.where(matched, 0, 1).astype(jnp.int32), stable=True).astype(jnp.int32)
            chosen = ordering[:most_rows]
            live_rows = jnp.sum(matched.astype(jnp.int32))
            occupied = positions < live_rows
            token_row = (chosen // TOPK).astype(jnp.int32)
            rows_x = jnp.where(occupied[:, None], x_m[token_row], jnp.zeros((), x_m.dtype))
            rows_dy = jnp.where(occupied[:, None], dy_m[token_row], jnp.zeros((), dy_m.dtype))
            rows_gate = jnp.where(occupied, gates_m[chosen], jnp.zeros((), gates_m.dtype))
            input_rows, gate_grad, pre_grad, up_grad, hidden, scaled_dy = expert_rows(rows_x, rows_dy, rows_gate, gate_w, up_w, down_w)
            in_acc = in_acc.at[token_row].add(jnp.where(occupied[:, None], input_rows.astype(jnp.float32), jnp.float32(0.0)))
            g_acc = g_acc.at[chosen].add(jnp.where(occupied, gate_grad.astype(jnp.float32), jnp.float32(0.0)))
            part_gate = jnp.dot(rows_x.T, pre_grad, preferred_element_type=jnp.float32)
            part_up = jnp.dot(rows_x.T, up_grad, preferred_element_type=jnp.float32)
            part_down = jnp.dot(hidden.T, scaled_dy, preferred_element_type=jnp.float32)
            rounded = lax.optimization_barrier((part_gate.astype(jnp.bfloat16), part_up.astype(jnp.bfloat16), part_down.astype(jnp.bfloat16)))
            totals = tuple(total + part.astype(jnp.float32) for total, part in zip(totals, rounded))
            return totals, (in_acc, g_acc)

        zeros_init = (jnp.zeros((D, FF), jnp.float32), jnp.zeros((D, FF), jnp.float32), jnp.zeros((FF, D), jnp.float32))
        totals, (input_acc, gates_acc) = lax.scan(one_member, zeros_init, (group_ids, group_x, group_dy, group_gates, input_acc, gates_acc))
        return (input_acc, gates_acc), tuple(total.astype(jnp.bfloat16) for total in totals)

    start_state = (jnp.zeros((N_DP, group_rows, D), jnp.float32), jnp.zeros((N_DP, group_rows * TOPK), jnp.float32))
    (input_acc, gates_acc), (grad_gate, grad_up, grad_down) = lax.scan(one_expert, start_state, jnp.arange(experts, dtype=jnp.int32))
    d_tokens = input_acc.reshape(N_DP * group_rows, D).astype(jnp.bfloat16)
    d_gates = gates_acc.reshape(N_DP * group_rows, TOPK).astype(jnp.bfloat16)
    return d_tokens, d_gates, grad_gate, grad_up, grad_down
```

```python
import functools

import jax
import jax.numpy as jnp
from jax import lax
from jax.experimental import pallas as pl
from jax.experimental.pallas import tpu as pltpu
from jax.sharding import PartitionSpec as P

MESH = pl.DeviceIdType.MESH
BF = jnp.bfloat16
F32 = jnp.float32

TOK = 160
TOP = 8
D = 2048
FF = 768
NE = 32
SLOT = 16
ROWS = NE * SLOT
GL = NE * SLOT
UNITS = 6
MSGS = 6
HALF = 128


def coords():
    dp, ex = lax.axis_index("dp"), lax.axis_index("expert")
    return dp % 4, ex // 8, (dp // 4) * 4 + (ex // 2) % 4, ex % 2


def device(x, y, z, c):
    z = (z + 8) % 8
    return {"dp": (z // 4) * 4 + (x + 4) % 4, "expert": (((y + 4) % 4) * 4 + z % 4) * 2 + c}


def offset(j):
    i = (j // 2) % 4
    return i, (i + j // 8) % 4, j % 2


def z_shift(kind, core):
    return jnp.where(kind == 1, 1, 0) - jnp.where(kind == 2, 1, 0) + jnp.where(kind == 3, 2 - 4 * core, 0)


def target(j):
    x, y, z, c = coords()
    dy, kind, dc = offset(j)
    return device(x, y + dy, z + z_shift(kind, c), (c + dc) % 2)


def origin(j):
    x, y, z, c = coords()
    dy, kind, dc = offset(j)
    c0 = (c + dc) % 2
    return device(x, y - dy, z - z_shift(kind, c0), c0)


def target_expert(j):
    x, y, z, c = coords()
    dy, kind, dc = offset(j)
    return (((y + dy) % 4) * 4 + (z + z_shift(kind, c) + 8) % 4) * 2 + (c + dc) % 2


def peers():
    x, y, z, c = coords()
    for dz in (0, 1, -1, 2, -2):
        for dy in range(4):
            for dc in (0, 1):
                if (dz, dy, dc) != (0, 0, 0):
                    yield device(x, y + dy, z + dz, (c + dc) % 2)
    yield device(x + 1, y, z, c)
    yield device(x - 1, y, z, c)
    yield device(x, y, z + 4, c)


def block(j):
    return pl.ds(pl.multiple_of(j * SLOT, SLOT), SLOT)


def iota(shape, dim):
    return lax.broadcasted_iota(jnp.int32, shape, dim)


def kernel(
    ids_ref, gate_ref, tok_ref, dy_ref, wg_hbm, wu_hbm, wd_hbm,
    dtok_ref, dgate_ref, owg_ref, owu_ref, owd_ref,
    wg, wu, wd, sent, xs, sel, gs, rt, back, dgs, rs_s, rs_r, own, z_s, z_r,
    w_sem, d_ss, d_rs, b_ss, b_rs, r_ss, r_rs, z_ss, z_rs,
):
    x, y, z, c = coords()
    me = lax.axis_index("expert")
    my_half = lax.axis_index("dp") // 4

    barrier = pltpu.get_barrier_semaphore()
    count = 0
    for peer in peers():
        pl.semaphore_signal(barrier, inc=1, device_id=peer, device_id_type=MESH)
        count += 1

    loads = [
        pltpu.make_async_copy(src.at[0], dst, w_sem.at[n])
        for n, (src, dst) in enumerate(((wg_hbm, wg), (wu_hbm, wu), (wd_hbm, wd)))
    ]
    for load in loads:
        load.start()

    expert_of = iota((TOK, GL), 1) // SLOT
    member = jnp.zeros((TOK, GL), F32)
    value = jnp.zeros((TOK, GL), F32)
    for k in range(TOP):
        hit = ids_ref[:, k : k + 1] == expert_of
        member = jnp.where(hit, 1.0, member)
        value = jnp.where(hit, gate_ref[:, k : k + 1].astype(F32), value)
    earlier = (iota((TOK, TOK), 1) < iota((TOK, TOK), 0)).astype(F32).astype(BF)
    rank = jnp.dot(earlier, member.astype(BF), preferred_element_type=F32)
    slot_of = (iota((TOK, GL), 1) % SLOT).astype(F32)
    chosen = jnp.where(rank == slot_of, member, 0.0)
    sel[...] = chosen.astype(BF)
    gate_row = jnp.sum(chosen * value, axis=0, keepdims=True)
    pick = chosen.T.astype(BF)
    last = iota((ROWS, 512), 0) % SLOT == SLOT - 1
    for p, ref in enumerate((tok_ref, dy_ref)):
        for n in range(D // 512):
            cols = pl.ds(n * 512, 512)
            rows = jnp.dot(pick, ref[:, cols], preferred_element_type=F32)
            if p == 0 and n == 0:
                rows = jnp.where(last, gate_row, rows)
            sent[p, :, cols] = rows.astype(BF)

    pl.semaphore_wait(barrier, count)

    def dispatch(p, j):
        return pltpu.make_async_remote_copy(
            src_ref=sent.at[p, block(target_expert(j))],
            dst_ref=xs.at[p, block(j)],
            send_sem=d_ss.at[p, j],
            recv_sem=d_rs.at[p, j],
            device_id=target(j),
            device_id_type=MESH,
        )

    @pl.loop(1, NE)
    def _(j):
        dispatch(0, j).start()
        dispatch(1, j).start()

    for p in range(2):
        xs[p, 0:SLOT, :] = sent[p, block(me), :]
    for load in loads:
        load.wait()

    @pl.loop(1, NE)
    def _(j):
        dispatch(0, j).wait_recv()
        dispatch(1, j).wait_recv()

    lane = iota((1, SLOT, GL), 2)
    mine = lane == me * SLOT + iota((1, SLOT, GL), 1)

    def expert(rows, count):
        row = xs[0, rows, 0:GL].astype(F32).reshape(count // SLOT, SLOT, GL)
        row = jnp.where(iota((1, SLOT, GL), 1) == SLOT - 1, row, 0.0)
        row = jnp.sum(row, axis=1, keepdims=True)
        scale = jnp.sum(jnp.where(mine, row, 0.0), axis=2, keepdims=True).reshape(count, 1)

        def part(f, total):
            cols = pl.ds(pl.multiple_of(f * 256, 256), 256)
            gate_pre = jnp.dot(xs[0, rows, :], wg[:, cols], preferred_element_type=F32)
            up_pre = jnp.dot(xs[0, rows, :], wu[:, cols], preferred_element_type=F32)
            raw = lax.dot_general(
                xs[1, rows, :], wd[cols, :], (((1,), (1,)), ((), ())), preferred_element_type=F32
            )
            sig = jax.nn.sigmoid(gate_pre)
            silu = gate_pre * sig
            hidden = (silu * up_pre).astype(BF)
            grad = scale * raw
            gs[2, rows, cols] = (grad * silu).astype(BF)
            gs[1, rows, cols] = (grad * up_pre * sig * (1.0 + gate_pre * (1.0 - sig))).astype(BF)
            gs[0, rows, cols] = hidden
            return total + jnp.sum(hidden.astype(F32) * raw, axis=1, keepdims=True)

        total = lax.fori_loop(0, FF // 256, part, jnp.zeros((count, 1), F32))
        grads = total.astype(BF).astype(F32).reshape(count // SLOT, SLOT, 1)
        grads = jnp.sum(jnp.where(mine, grads, 0.0), axis=1, keepdims=True)
        grads = jnp.broadcast_to(grads, (count // SLOT, SLOT, GL)).reshape(count, GL)
        dgs[rows, :] = grads.astype(BF)
        xs[1, rows, :] = (scale * xs[1, rows, :].astype(F32)).astype(BF)

    @pl.loop(0, 2)
    def _(m):
        expert(pl.ds(pl.multiple_of(m * 256, 256), 256), 256)

    def half_of(u):
        return jnp.where(u < 3, 1 - my_half, my_half)

    def tile(u, to_x, half):
        kind = u % 3
        start = (half_of(u) * 4 + (to_x + 4) % 4) * 256 + half * HALF
        left = xs[jnp.where(kind == 0, 1, 0), :, pl.ds(pl.multiple_of(start, HALF), HALF)]
        return lax.dot_general(
            left, gs[kind], (((0,), (0,)), ((), ())), preferred_element_type=F32
        )

    def message(u, m):
        step = 1 if m % 2 == 0 else -1
        return pltpu.make_async_remote_copy(
            src_ref=rs_s.at[u * MSGS + m],
            dst_ref=rs_r.at[u * MSGS + m],
            send_sem=r_ss.at[u * MSGS + m],
            recv_sem=r_rs.at[u * MSGS + m],
            device_id=device(x + step, y, z, c),
            device_id_type=MESH,
        )

    def send(u, m, tile_value):
        rs_s[u * MSGS + m] = tile_value.astype(BF)
        message(u, m).start()

    def received(u, m):
        message(u, m).wait_recv()
        return rs_r[u * MSGS + m].astype(F32)

    def to_partner(n, half):
        return pltpu.make_async_remote_copy(
            src_ref=z_s.at[n * 2 + half],
            dst_ref=z_r.at[n * 2 + half],
            send_sem=z_ss.at[n * 2 + half],
            recv_sem=z_rs.at[n * 2 + half],
            device_id=device(x, y, z + 4, c),
            device_id_type=MESH,
        )

    def give_back(j):
        return pltpu.make_async_remote_copy(
            src_ref=rt.at[block(j)],
            dst_ref=back.at[block(me)],
            send_sem=b_ss.at[j],
            recv_sem=b_rs.at[j],
            device_id=origin(j),
            device_id_type=MESH,
        )

    def returns():
        ends = iota((ROWS, 512), 0) % SLOT == SLOT - 1

        @pl.loop(0, D // 512)
        def _(n):
            feats = pl.ds(pl.multiple_of(n * 512, 512), 512)
            contract = (((1,), (1,)), ((), ()))
            rows = lax.dot_general(gs[1], wg[feats, :], contract, preferred_element_type=F32)
            rows = rows + lax.dot_general(gs[2], wu[feats, :], contract, preferred_element_type=F32)
            rt[:, feats] = rows.astype(BF)

        rt[:, 0:GL] = jnp.where(ends, dgs[...].astype(F32), rt[:, 0:GL].astype(F32)).astype(BF)

        @pl.loop(1, NE)
        def _(j):
            give_back(j).start()

        back[block(me), :] = rt[0:SLOT, :]

    @pl.loop(0, UNITS + 2)
    def _(v):
        @pl.when(v < UNITS)
        def _():
            u = v
            send(u, 0, tile(u, x + 2, 0))
            send(u, 1, tile(u, x + 2, 1))
            send(u, 2, tile(u, x + 1, 1))
            send(u, 3, tile(u, x - 1, 0))

        @pl.when(v == 1)
        def _():
            returns()

        @pl.when((v >= 1) & (v < UNITS + 1))
        def _():
            u = v - 1
            send(u, 4, tile(u, x + 1, 0) + received(u, 0))
            send(u, 5, tile(u, x - 1, 1) + received(u, 1))

        @pl.when(v >= 2)
        def _():
            u = v - 2
            for half in range(2):
                total = tile(u, x, half) + received(u, 4 + half) + received(u, 3 - half)

                @pl.when(u < 3)
                def _():
                    z_s[u * 2 + half] = total.astype(BF)
                    to_partner(u, half).start()

                @pl.when(u >= 3)
                def _():
                    own[(u - 3) * 2 + half] = total

    @pl.loop(1, NE)
    def _(j):
        give_back(j).wait_recv()

    for n in range(D // 512):
        cols = pl.ds(n * 512, 512)
        dtok_ref[:, cols] = jnp.dot(sel[...], back[:, cols], preferred_element_type=F32).astype(BF)
    ends = iota((ROWS, GL), 0) % SLOT == SLOT - 1
    row = jnp.sum(jnp.where(ends, back[:, 0:GL].astype(F32), 0.0), axis=0, keepdims=True)
    picked = sel[...].astype(F32) * row
    at = iota((TOK, TOP), 1)
    grads = jnp.zeros((TOK, TOP), F32)
    for k in range(TOP):
        hit = ids_ref[:, k : k + 1] == expert_of
        one = jnp.sum(jnp.where(hit, picked, 0.0), axis=1, keepdims=True)
        grads = jnp.where(at == k, one, grads)
    dgate_ref[...] = grads.astype(BF)

    for n, ref in enumerate((owd_ref, owg_ref, owu_ref)):
        for half in range(2):
            to_partner(n, half).wait_recv()
            total = own[n * 2 + half] + z_r[n * 2 + half].astype(F32)
            if n == 0:
                ref[0, :, half * HALF : (half + 1) * HALF] = total.T.astype(BF)
            else:
                ref[0, half * HALF : (half + 1) * HALF, :] = total.astype(BF)

    @pl.loop(1, NE)
    def _(j):
        dispatch(0, j).wait_send()
        dispatch(1, j).wait_send()
        give_back(j).wait_send()

    @pl.loop(0, UNITS)
    def _(u):
        for m in range(MSGS):
            message(u, m).wait_send()

    for n in range(3):
        for half in range(2):
            to_partner(n, half).wait_send()


def body(tokens, out_grad, expert_ids, gate_vals, w_gate, w_up, w_down):
    vmem = pl.BlockSpec(memory_space=pltpu.VMEM)
    hbm = pl.BlockSpec(memory_space=pl.ANY)
    dma = pltpu.SemaphoreType.DMA
    return pl.pallas_call(
        kernel,
        out_shape=(
            jax.ShapeDtypeStruct((TOK, D), BF),
            jax.ShapeDtypeStruct((TOK, TOP), BF),
            jax.ShapeDtypeStruct((1, 256, FF), BF),
            jax.ShapeDtypeStruct((1, 256, FF), BF),
            jax.ShapeDtypeStruct((1, FF, 256), BF),
        ),
        in_specs=[vmem] * 4 + [hbm] * 3,
        out_specs=[vmem] * 5,
        scratch_shapes=[
            pltpu.VMEM((D, FF), BF),
            pltpu.VMEM((D, FF), BF),
            pltpu.VMEM((FF, D), BF),
            pltpu.VMEM((2, ROWS, D), BF),
            pltpu.VMEM((2, ROWS, D), BF),
            pltpu.VMEM((TOK, GL), BF),
            pltpu.VMEM((3, ROWS, FF), BF),
            pltpu.VMEM((ROWS, D), BF),
            pltpu.VMEM((ROWS, D), BF),
            pltpu.VMEM((ROWS, GL), BF),
            pltpu.VMEM((UNITS * MSGS, HALF, FF), BF),
            pltpu.VMEM((UNITS * MSGS, HALF, FF), BF),
            pltpu.VMEM((6, HALF, FF), F32),
            pltpu.VMEM((6, HALF, FF), BF),
            pltpu.VMEM((6, HALF, FF), BF),
            dma((3,)),
            dma((2, NE)),
            dma((2, NE)),
            dma((NE,)),
            dma((NE,)),
            dma((UNITS * MSGS,)),
            dma((UNITS * MSGS,)),
            dma((6,)),
            dma((6,)),
        ],
        compiler_params=pltpu.CompilerParams(
            collective_id=0, has_side_effects=True, vmem_limit_bytes=60 * 2**20
        ),
    )(expert_ids, gate_vals, tokens, out_grad, w_gate, w_up, w_down)


def solution(mesh):
    in_specs = (
        P(("dp", "expert"), None),
        P(("dp", "expert"), None),
        P(("dp", "expert"), None),
        P(("dp", "expert"), None),
        P("expert", None, None),
        P("expert", None, None),
        P("expert", None, None),
    )
    out_specs = (
        P(("dp", "expert"), None),
        P(("dp", "expert"), None),
        P("expert", "dp", None),
        P("expert", "dp", None),
        P("expert", None, "dp"),
    )
    return jax.shard_map(body, mesh=mesh, in_specs=in_specs, out_specs=out_specs, check_vma=False)
```

```python
import functools

import jax
import jax.numpy as jnp
from jax import lax
from jax.experimental import pallas as pl
from jax.experimental.pallas import tpu as pltpu
from jax.sharding import PartitionSpec as P

MESH = pl.DeviceIdType.MESH
BF = jnp.bfloat16
F32 = jnp.float32

TOK = 160
TOP = 8
D = 2048
FF = 768
NE = 32
SLOT = 16
ROWS = NE * SLOT
GL = NE * SLOT
UNITS = 6
MSGS = 6
HALF = 128
FIRST = 14
RELAYS = NE - FIRST
CHUNKS = ((0, 224), (224, 144), (368, 144))


def coords():
    dp, ex = lax.axis_index("dp"), lax.axis_index("expert")
    return dp % 4, ex // 8, (dp // 4) * 4 + (ex // 2) % 4, ex % 2


def device(x, y, z, c):
    z = (z + 8) % 8
    return {"dp": (z // 4) * 4 + (x + 4) % 4, "expert": (((y + 4) % 4) * 4 + z % 4) * 2 + c}


def offset(j):
    q, r = j // 2, (j - FIRST) // 2
    plain = j < FIRST
    dy = jnp.where(plain, jnp.where(q < 4, q, 0), 1 + r % 3)
    kind = jnp.where(plain, jnp.where(q < 4, 0, q - 3), 1 + (r % 3 + r // 3) % 3)
    return dy, kind, j % 2


def z_shift(kind, core):
    return jnp.where(kind == 1, 1, 0) - jnp.where(kind == 2, 1, 0) + jnp.where(kind == 3, 2 - 4 * core, 0)


def target(j):
    x, y, z, c = coords()
    dy, kind, dc = offset(j)
    return device(x, y + dy, z + z_shift(kind, c), (c + dc) % 2)


def origin(j):
    x, y, z, c = coords()
    dy, kind, dc = offset(j)
    c0 = (c + dc) % 2
    return device(x, y - dy, z - z_shift(kind, c0), c0)


def target_expert(j):
    x, y, z, c = coords()
    dy, kind, dc = offset(j)
    return (((y + dy) % 4) * 4 + (z + z_shift(kind, c) + 8) % 4) * 2 + (c + dc) % 2


def turn(j, p, second):
    x, y, z, c = coords()
    dy, kind, dc = offset(j)
    if second == (p == 0):
        return device(x, y + dy, z, c)
    return device(x, y, z + z_shift(kind, c), (c + dc) % 2)


def peers():
    x, y, z, c = coords()
    for dz in (0, 1, -1, 2, -2):
        for dy in range(4):
            for dc in (0, 1):
                if (dz, dy, dc) != (0, 0, 0):
                    yield device(x, y + dy, z + dz, (c + dc) % 2)
    yield device(x + 1, y, z, c)
    yield device(x - 1, y, z, c)
    yield device(x, y, z + 4, c)


def block(j):
    return pl.ds(pl.multiple_of(j * SLOT, SLOT), SLOT)


def iota(shape, dim):
    return lax.broadcasted_iota(jnp.int32, shape, dim)


def kernel(
    ids_ref, gate_ref, tok_ref, dy_ref, wg_hbm, wu_hbm, wd_hbm,
    dtok_ref, dgate_ref, owg_ref, owu_ref, owd_ref,
    wg, wu, wd, sent, relay, xs, sel, gs, rt, back, dgs, rs_s, rs_r, own, z_s, z_r,
    w_sem, h_ss, h_rs, d_ss, d_rs, b_ss, b_rs, r_ss, r_rs, z_ss, z_rs,
):
    x, y, z, c = coords()
    me = lax.axis_index("expert")
    my_half = lax.axis_index("dp") // 4

    barrier = pltpu.get_barrier_semaphore()
    count = 0
    for peer in peers():
        pl.semaphore_signal(barrier, inc=1, device_id=peer, device_id_type=MESH)
        count += 1

    loads = [
        pltpu.make_async_copy(src.at[0], dst, w_sem.at[n])
        for n, (src, dst) in enumerate(((wg_hbm, wg), (wu_hbm, wu), (wd_hbm, wd)))
    ]
    for load in loads:
        load.start()

    expert_of = iota((TOK, GL), 1) // SLOT
    ids = ids_ref[...].T
    gates = gate_ref[...].astype(F32).T
    member = jnp.zeros((TOK, GL), F32)
    value = jnp.zeros((TOK, GL), F32)
    for k in range(TOP):
        hit = ids[:, k : k + 1] == expert_of
        member = jnp.where(hit, 1.0, member)
        value = jnp.where(hit, gates[:, k : k + 1], value)
    earlier = (iota((TOK, TOK), 1) < iota((TOK, TOK), 0)).astype(F32).astype(BF)
    rank = jnp.dot(earlier, member.astype(BF), preferred_element_type=F32)
    slot_of = (iota((TOK, GL), 1) % SLOT).astype(F32)
    chosen = jnp.where(rank == slot_of, member, 0.0)
    sel[...] = chosen.astype(BF)
    gate_row = jnp.sum(chosen * value, axis=0, keepdims=True)
    pick = chosen.T.astype(BF)
    last = iota((ROWS, 512), 0) % SLOT == SLOT - 1
    for p, ref in enumerate((tok_ref, dy_ref)):
        for n in range(D // 512):
            cols = pl.ds(n * 512, 512)
            rows = jnp.dot(pick, ref[:, cols], preferred_element_type=F32)
            if p == 0 and n == 0:
                rows = jnp.where(last, gate_row, rows)
            sent[p, :, cols] = rows.astype(BF)

    pl.semaphore_wait(barrier, count)

    def arrival(p, j, src, to):
        return pltpu.make_async_remote_copy(
            src_ref=src,
            dst_ref=xs.at[p, block(j)],
            send_sem=d_ss.at[p, j],
            recv_sem=d_rs.at[p, j],
            device_id=to,
            device_id_type=MESH,
        )

    def direct(p, j):
        return arrival(p, j, sent.at[p, block(target_expert(j))], target(j))

    def hop(p, r):
        j = r + FIRST
        return pltpu.make_async_remote_copy(
            src_ref=sent.at[p, block(target_expert(j))],
            dst_ref=relay.at[p, block(r)],
            send_sem=h_ss.at[p, r],
            recv_sem=h_rs.at[p, r],
            device_id=turn(j, p, False),
            device_id_type=MESH,
        )

    def onward(p, r):
        j = r + FIRST
        return arrival(p, j, relay.at[p, block(r)], turn(j, p, True))

    @pl.loop(0, RELAYS)
    def _(r):
        hop(0, r).start()
        hop(1, r).start()

    @pl.loop(1, FIRST)
    def _(j):
        direct(0, j).start()
        direct(1, j).start()

    for p in range(2):
        xs[p, 0:SLOT, :] = sent[p, block(me), :]
    for load in loads:
        load.wait()

    @pl.loop(0, RELAYS)
    def _(r):
        for p in range(2):
            hop(p, r).wait_recv()
            onward(p, r).start()

    @pl.loop(1, FIRST)
    def _(j):
        direct(0, j).wait_recv()
        direct(1, j).wait_recv()

    lane = iota((1, SLOT, GL), 2)
    mine = lane == me * SLOT + iota((1, SLOT, GL), 1)

    def expert(rows, count):
        row = xs[0, rows, 0:GL].astype(F32).reshape(count // SLOT, SLOT, GL)
        row = jnp.where(iota((1, SLOT, GL), 1) == SLOT - 1, row, 0.0)
        row = jnp.sum(row, axis=1, keepdims=True)
        scale = jnp.sum(jnp.where(mine, row, 0.0), axis=2, keepdims=True).reshape(count, 1)

        def part(f, total):
            cols = pl.ds(pl.multiple_of(f * 256, 256), 256)
            gate_pre = jnp.dot(xs[0, rows, :], wg[:, cols], preferred_element_type=F32)
            up_pre = jnp.dot(xs[0, rows, :], wu[:, cols], preferred_element_type=F32)
            raw = lax.dot_general(
                xs[1, rows, :], wd[cols, :], (((1,), (1,)), ((), ())), preferred_element_type=F32
            )
            sig = jax.nn.sigmoid(gate_pre)
            silu = gate_pre * sig
            hidden = (silu * up_pre).astype(BF)
            grad = scale * raw
            gs[2, rows, cols] = (grad * silu).astype(BF)
            gs[1, rows, cols] = (grad * up_pre * sig * (1.0 + gate_pre * (1.0 - sig))).astype(BF)
            gs[0, rows, cols] = hidden
            return total + jnp.sum(hidden.astype(F32) * raw, axis=1, keepdims=True)

        total = lax.fori_loop(0, FF // 256, part, jnp.zeros((count, 1), F32))
        grads = total.astype(BF).astype(F32).reshape(count // SLOT, SLOT, 1)
        grads = jnp.sum(jnp.where(mine, grads, 0.0), axis=1, keepdims=True)
        grads = jnp.broadcast_to(grads, (count // SLOT, SLOT, GL)).reshape(count, GL)
        dgs[rows, :] = grads.astype(BF)
        xs[1, rows, :] = (scale * xs[1, rows, :].astype(F32)).astype(BF)

    def input_rows(rows, count):
        ends = iota((count, GL), 0) % SLOT == SLOT - 1

        @pl.loop(0, D // 512)
        def _(n):
            feats = pl.ds(pl.multiple_of(n * 512, 512), 512)
            contract = (((1,), (1,)), ((), ()))
            out = lax.dot_general(gs[1, rows, :], wg[feats, :], contract, preferred_element_type=F32)
            out = out + lax.dot_general(
                gs[2, rows, :], wu[feats, :], contract, preferred_element_type=F32
            )
            rt[rows, feats] = out.astype(BF)

        rt[rows, 0:GL] = jnp.where(ends, dgs[rows, :].astype(F32), rt[rows, 0:GL].astype(F32)).astype(BF)

    def give_back(j):
        return pltpu.make_async_remote_copy(
            src_ref=rt.at[block(j)],
            dst_ref=back.at[block(me)],
            send_sem=b_ss.at[j],
            recv_sem=b_rs.at[j],
            device_id=origin(j),
            device_id_type=MESH,
        )

    def return_blocks(start, count):
        @pl.loop(max(start // SLOT, 1), (start + count) // SLOT)
        def _(j):
            give_back(j).start()

    for n, (start, count) in enumerate(CHUNKS):
        if n > 0:
            @pl.loop(start // SLOT, (start + count) // SLOT)
            def _(j):
                onward(0, j - FIRST).wait_recv()
                onward(1, j - FIRST).wait_recv()
        if n == len(CHUNKS) - 1:
            return_blocks(0, start)
            back[block(me), :] = rt[0:SLOT, :]
        expert(pl.ds(start, count), count)
        if n < len(CHUNKS) - 1:
            input_rows(pl.ds(start, count), count)

    def half_of(u):
        return jnp.where(u < 3, 1 - my_half, my_half)

    def tile(u, to_x, half):
        kind = u % 3
        start = (half_of(u) * 4 + (to_x + 4) % 4) * 256 + half * HALF
        left = xs[jnp.where(kind == 0, 1, 0), :, pl.ds(pl.multiple_of(start, HALF), HALF)]
        return lax.dot_general(
            left, gs[kind], (((0,), (0,)), ((), ())), preferred_element_type=F32
        )

    def message(u, m):
        step = 1 if m % 2 == 0 else -1
        return pltpu.make_async_remote_copy(
            src_ref=rs_s.at[u * MSGS + m],
            dst_ref=rs_r.at[u * MSGS + m],
            send_sem=r_ss.at[u * MSGS + m],
            recv_sem=r_rs.at[u * MSGS + m],
            device_id=device(x + step, y, z, c),
            device_id_type=MESH,
        )

    def send(u, m, tile_value):
        rs_s[u * MSGS + m] = tile_value.astype(BF)
        message(u, m).start()

    def received(u, m):
        message(u, m).wait_recv()
        return rs_r[u * MSGS + m].astype(F32)

    def to_partner(n, half):
        return pltpu.make_async_remote_copy(
            src_ref=z_s.at[n * 2 + half],
            dst_ref=z_r.at[n * 2 + half],
            send_sem=z_ss.at[n * 2 + half],
            recv_sem=z_rs.at[n * 2 + half],
            device_id=device(x, y, z + 4, c),
            device_id_type=MESH,
        )

    @pl.loop(0, UNITS + 2)
    def _(v):
        @pl.when(v < UNITS)
        def _():
            u = v
            send(u, 0, tile(u, x + 2, 0))
            send(u, 1, tile(u, x + 2, 1))
            send(u, 2, tile(u, x + 1, 1))
            send(u, 3, tile(u, x - 1, 0))

        @pl.when(v == 1)
        def _():
            start, count = CHUNKS[-1]
            input_rows(pl.ds(start, count), count)
            return_blocks(start, count)

        @pl.when((v >= 1) & (v < UNITS + 1))
        def _():
            u = v - 1
            send(u, 4, tile(u, x + 1, 0) + received(u, 0))
            send(u, 5, tile(u, x - 1, 1) + received(u, 1))

        @pl.when(v >= 2)
        def _():
            u = v - 2
            for half in range(2):
                total = tile(u, x, half) + received(u, 4 + half) + received(u, 3 - half)

                @pl.when(u < 3)
                def _():
                    z_s[u * 2 + half] = total.astype(BF)
                    to_partner(u, half).start()

                @pl.when(u >= 3)
                def _():
                    own[(u - 3) * 2 + half] = total

    @pl.loop(1, NE)
    def _(j):
        give_back(j).wait_recv()

    for n in range(D // 512):
        cols = pl.ds(n * 512, 512)
        dtok_ref[:, cols] = jnp.dot(sel[...], back[:, cols], preferred_element_type=F32).astype(BF)
    ends = iota((ROWS, GL), 0) % SLOT == SLOT - 1
    row = jnp.sum(jnp.where(ends, back[:, 0:GL].astype(F32), 0.0), axis=0, keepdims=True)
    picked = sel[...].astype(F32) * row
    at = iota((TOK, TOP), 1)
    grads = jnp.zeros((TOK, TOP), F32)
    for k in range(TOP):
        hit = ids[:, k : k + 1] == expert_of
        one = jnp.sum(jnp.where(hit, picked, 0.0), axis=1, keepdims=True)
        grads = jnp.where(at == k, one, grads)
    dgate_ref[...] = grads.T.astype(BF)

    for n, ref in enumerate((owd_ref, owg_ref, owu_ref)):
        for half in range(2):
            to_partner(n, half).wait_recv()
            total = own[n * 2 + half] + z_r[n * 2 + half].astype(F32)
            if n == 0:
                ref[0, :, half * HALF : (half + 1) * HALF] = total.T.astype(BF)
            else:
                ref[0, half * HALF : (half + 1) * HALF, :] = total.astype(BF)

    @pl.loop(1, NE)
    def _(j):
        direct(0, j).wait_send()
        direct(1, j).wait_send()
        give_back(j).wait_send()

    @pl.loop(0, RELAYS)
    def _(r):
        hop(0, r).wait_send()
        hop(1, r).wait_send()

    @pl.loop(0, UNITS)
    def _(u):
        for m in range(MSGS):
            message(u, m).wait_send()

    for n in range(3):
        for half in range(2):
            to_partner(n, half).wait_send()


def settle(*refs):
    n = (len(refs) - 2) // 3
    ins, outs, bufs, in_sem, out_sem = refs[:n], refs[n : 2 * n], refs[2 * n : 3 * n], refs[-2], refs[-1]
    takes = [pltpu.make_async_copy(ins[i], bufs[i], in_sem.at[i]) for i in range(n)]
    puts = [pltpu.make_async_copy(bufs[i], outs[i], out_sem.at[i]) for i in range(n)]
    for take in takes:
        take.start()
    for take, put in zip(takes, puts):
        take.wait()
        put.start()
    for put in puts:
        put.wait()


def body(tokens, out_grad, expert_ids, gate_vals, w_gate, w_up, w_down):
    vmem = pl.BlockSpec(memory_space=pltpu.VMEM)
    hbm = pl.BlockSpec(memory_space=pl.ANY)
    dma = pltpu.SemaphoreType.DMA
    shapes = (
        jax.ShapeDtypeStruct((TOK, D), BF),
        jax.ShapeDtypeStruct((TOP, TOK), BF),
        jax.ShapeDtypeStruct((1, 256, FF), BF),
        jax.ShapeDtypeStruct((1, 256, FF), BF),
        jax.ShapeDtypeStruct((1, FF, 256), BF),
    )
    outs = pl.pallas_call(
        kernel,
        out_shape=shapes,
        in_specs=[vmem] * 4 + [hbm] * 3,
        out_specs=[vmem] * 5,
        scratch_shapes=[
            pltpu.VMEM((D, FF), BF),
            pltpu.VMEM((D, FF), BF),
            pltpu.VMEM((FF, D), BF),
            pltpu.VMEM((2, ROWS, D), BF),
            pltpu.VMEM((2, RELAYS * SLOT, D), BF),
            pltpu.VMEM((2, ROWS, D), BF),
            pltpu.VMEM((TOK, GL), BF),
            pltpu.VMEM((3, ROWS, FF), BF),
            pltpu.VMEM((ROWS, D), BF),
            pltpu.VMEM((ROWS, D), BF),
            pltpu.VMEM((ROWS, GL), BF),
            pltpu.VMEM((UNITS * MSGS, HALF, FF), BF),
            pltpu.VMEM((UNITS * MSGS, HALF, FF), BF),
            pltpu.VMEM((6, HALF, FF), F32),
            pltpu.VMEM((6, HALF, FF), BF),
            pltpu.VMEM((6, HALF, FF), BF),
            dma((3,)),
            dma((2, RELAYS)),
            dma((2, RELAYS)),
            dma((2, NE)),
            dma((2, NE)),
            dma((NE,)),
            dma((NE,)),
            dma((UNITS * MSGS,)),
            dma((UNITS * MSGS,)),
            dma((6,)),
            dma((6,)),
        ],
        compiler_params=pltpu.CompilerParams(
            collective_id=0, has_side_effects=True, vmem_limit_bytes=60 * 2**20
        ),
    )(expert_ids.T, gate_vals.T, tokens, out_grad, w_gate, w_up, w_down)
    d_tokens, d_gates, d_gate, d_up, d_down = pl.pallas_call(
        settle,
        out_shape=shapes,
        in_specs=[hbm] * 5,
        out_specs=[hbm] * 5,
        scratch_shapes=[pltpu.VMEM(s.shape, s.dtype) for s in shapes] + [dma((5,)), dma((5,))],
        compiler_params=pltpu.CompilerParams(vmem_limit_bytes=60 * 2**20),
    )(*outs)
    return d_tokens, d_gates.T, d_gate, d_up, d_down


def solution(mesh):
    in_specs = (
        P(("dp", "expert"), None),
        P(("dp", "expert"), None),
        P(("dp", "expert"), None),
        P(("dp", "expert"), None),
        P("expert", None, None),
        P("expert", None, None),
        P("expert", None, None),
    )
    out_specs = (
        P(("dp", "expert"), None),
        P(("dp", "expert"), None),
        P("expert", "dp", None),
        P("expert", "dp", None),
        P("expert", None, "dp"),
    )
    return jax.shard_map(body, mesh=mesh, in_specs=in_specs, out_specs=out_specs, check_vma=False)
```

```python
import functools

import jax
import jax.numpy as jnp
from jax import lax
from jax.experimental import pallas as pl
from jax.experimental.pallas import tpu as pltpu
from jax.sharding import PartitionSpec as P

MESH = pl.DeviceIdType.MESH
BF = jnp.bfloat16
F32 = jnp.float32

TOK = 160
TOP = 8
D = 2048
FF = 768
NE = 32
SLOT = 16
ROWS = NE * SLOT
GL = NE * SLOT
UNITS = 6
MSGS = 6
HALF = 128
FIRST = 14
RELAYS = NE - FIRST
CHUNKS = ((0, 224), (224, 208), (432, 80))
LAST = CHUNKS[2][0] // SLOT


def coords():
    dp, ex = lax.axis_index("dp"), lax.axis_index("expert")
    return dp % 4, ex // 8, (dp // 4) * 4 + (ex // 2) % 4, ex % 2


def device(x, y, z, c):
    z = (z + 8) % 8
    return {"dp": (z // 4) * 4 + (x + 4) % 4, "expert": (((y + 4) % 4) * 4 + z % 4) * 2 + c}


def offset(j):
    q, r = j // 2, (j - FIRST) // 2
    plain = j < FIRST
    dy = jnp.where(plain, jnp.where(q < 4, q, 0), 1 + r % 3)
    kind = jnp.where(plain, jnp.where(q < 4, 0, q - 3), 1 + (r % 3 + r // 3) % 3)
    return dy, kind, j % 2


def z_shift(kind, core):
    return jnp.where(kind == 1, 1, 0) - jnp.where(kind == 2, 1, 0) + jnp.where(kind == 3, 2 - 4 * core, 0)


def target(j):
    x, y, z, c = coords()
    dy, kind, dc = offset(j)
    return device(x, y + dy, z + z_shift(kind, c), (c + dc) % 2)


def origin(j):
    x, y, z, c = coords()
    dy, kind, dc = offset(j)
    c0 = (c + dc) % 2
    return device(x, y - dy, z - z_shift(kind, c0), c0)


def target_expert(j):
    x, y, z, c = coords()
    dy, kind, dc = offset(j)
    return (((y + dy) % 4) * 4 + (z + z_shift(kind, c) + 8) % 4) * 2 + (c + dc) % 2


def turn(j, p, second):
    x, y, z, c = coords()
    dy, kind, dc = offset(j)
    if second == (p == 0):
        return device(x, y + dy, z, c)
    return device(x, y, z + z_shift(kind, c), (c + dc) % 2)


def peers():
    x, y, z, c = coords()
    for dz in (0, 1, -1, 2, -2):
        for dy in range(4):
            for dc in (0, 1):
                if (dz, dy, dc) != (0, 0, 0):
                    yield device(x, y + dy, z + dz, (c + dc) % 2)
    yield device(x + 1, y, z, c)
    yield device(x - 1, y, z, c)
    yield device(x, y, z + 4, c)


def block(j):
    return pl.ds(pl.multiple_of(j * SLOT, SLOT), SLOT)


def iota(shape, dim):
    return lax.broadcasted_iota(jnp.int32, shape, dim)


def kernel(
    ids_hbm, gate_hbm, tok_hbm, dy_hbm, wg_hbm, wu_hbm, wd_hbm,
    dtok_ref, dgate_ref, owg_ref, owu_ref, owd_ref,
    ids_ref, gate_ref, tok_ref, dy_ref, wg, wu, wd, sent, relay, xs, sel, gs, rt, back, dgs, rs_s, rs_r, own, z_s, z_r,
    w_sem, h_ss, h_rs, d_ss, d_rs, b_ss, b_rs, r_ss, r_rs, z_ss, z_rs,
):
    x, y, z, c = coords()
    me = lax.axis_index("expert")
    my_half = lax.axis_index("dp") // 4

    barrier = pltpu.get_barrier_semaphore()
    count = 0
    for peer in peers():
        pl.semaphore_signal(barrier, inc=1, device_id=peer, device_id_type=MESH)
        count += 1

    loads = [
        pltpu.make_async_copy(src, dst, w_sem.at[n])
        for n, (src, dst) in enumerate(
            ((ids_hbm, ids_ref), (gate_hbm, gate_ref), (tok_hbm, tok_ref), (dy_hbm, dy_ref), (wg_hbm.at[0], wg), (wu_hbm.at[0], wu), (wd_hbm.at[0], wd))
        )
    ]
    for load in loads:
        load.start()

    expert_of = iota((TOK, GL), 1) // SLOT
    loads[0].wait()
    loads[1].wait()
    ids = ids_ref[...].T
    gates = gate_ref[...].astype(F32).T
    member = jnp.zeros((TOK, GL), F32)
    value = jnp.zeros((TOK, GL), F32)
    for k in range(TOP):
        hit = ids[:, k : k + 1] == expert_of
        member = jnp.where(hit, 1.0, member)
        value = jnp.where(hit, gates[:, k : k + 1], value)
    earlier = (iota((TOK, TOK), 1) < iota((TOK, TOK), 0)).astype(F32).astype(BF)
    rank = jnp.dot(earlier, member.astype(BF), preferred_element_type=F32)
    slot_of = (iota((TOK, GL), 1) % SLOT).astype(F32)
    chosen = jnp.where(rank == slot_of, member, 0.0)
    sel[...] = chosen.astype(BF)
    gate_row = jnp.sum(chosen * value, axis=0, keepdims=True)
    pick = chosen.T.astype(BF)
    last = iota((ROWS, 512), 0) % SLOT == SLOT - 1
    for p, ref in enumerate((tok_ref, dy_ref)):
        loads[2 + p].wait()
        for n in range(D // 512):
            cols = pl.ds(n * 512, 512)
            rows = jnp.dot(pick, ref[:, cols], preferred_element_type=F32)
            if p == 0 and n == 0:
                rows = jnp.where(last, gate_row, rows)
            sent[p, :, cols] = rows.astype(BF)

    pl.semaphore_wait(barrier, count)

    def arrival(p, j, src, to):
        return pltpu.make_async_remote_copy(
            src_ref=src,
            dst_ref=xs.at[p, block(j)],
            send_sem=d_ss,
            recv_sem=d_rs.at[jnp.where(j < FIRST, 0, jnp.where(j < LAST, 1, 2))],
            device_id=to,
            device_id_type=MESH,
        )

    def direct(p, j):
        return arrival(p, j, sent.at[p, block(target_expert(j))], target(j))

    def hop(p, r):
        j = r + FIRST
        return pltpu.make_async_remote_copy(
            src_ref=sent.at[p, block(target_expert(j))],
            dst_ref=relay.at[p, block(r)],
            send_sem=h_ss,
            recv_sem=h_rs.at[p, r],
            device_id=turn(j, p, False),
            device_id_type=MESH,
        )

    def onward(p, r):
        j = r + FIRST
        return arrival(p, j, relay.at[p, block(r)], turn(j, p, True))

    @pl.loop(0, RELAYS)
    def _(r):
        hop(0, r).start()
        hop(1, r).start()

    @pl.loop(1, FIRST)
    def _(j):
        direct(0, j).start()
        direct(1, j).start()

    for p in range(2):
        xs[p, 0:SLOT, :] = sent[p, block(me), :]
    for load in loads[4:]:
        load.wait()

    @pl.loop(0, RELAYS)
    def _(r):
        for p in range(2):
            hop(p, r).wait_recv()
            onward(p, r).start()

    lane = iota((1, SLOT, GL), 2)
    mine = lane == me * SLOT + iota((1, SLOT, GL), 1)

    def expert(rows, count):
        row = xs[0, rows, 0:GL].astype(F32).reshape(count // SLOT, SLOT, GL)
        row = jnp.where(iota((1, SLOT, GL), 1) == SLOT - 1, row, 0.0)
        row = jnp.sum(row, axis=1, keepdims=True)
        scale = jnp.sum(jnp.where(mine, row, 0.0), axis=2, keepdims=True).reshape(count, 1)

        def part(f, total):
            cols = pl.ds(pl.multiple_of(f * 256, 256), 256)
            gate_pre = jnp.dot(xs[0, rows, :], wg[:, cols], preferred_element_type=F32)
            up_pre = jnp.dot(xs[0, rows, :], wu[:, cols], preferred_element_type=F32)
            raw = lax.dot_general(
                xs[1, rows, :], wd[cols, :], (((1,), (1,)), ((), ())), preferred_element_type=F32
            )
            sig = jax.nn.sigmoid(gate_pre)
            silu = gate_pre * sig
            hidden = (silu * up_pre).astype(BF)
            grad = scale * raw
            gs[2, rows, cols] = (grad * silu).astype(BF)
            gs[1, rows, cols] = (grad * up_pre * sig * (1.0 + gate_pre * (1.0 - sig))).astype(BF)
            gs[0, rows, cols] = hidden
            return total + jnp.sum(hidden.astype(F32) * raw, axis=1, keepdims=True)

        total = lax.fori_loop(0, FF // 256, part, jnp.zeros((count, 1), F32))
        grads = total.astype(BF).astype(F32).reshape(count // SLOT, SLOT, 1)
        grads = jnp.sum(jnp.where(mine, grads, 0.0), axis=1, keepdims=True)
        grads = jnp.broadcast_to(grads, (count // SLOT, SLOT, GL)).reshape(count, GL)
        dgs[rows, :] = grads.astype(BF)
        xs[1, rows, :] = (scale * xs[1, rows, :].astype(F32)).astype(BF)

    def input_rows(rows, count):
        ends = iota((count, GL), 0) % SLOT == SLOT - 1

        @pl.loop(0, D // 512)
        def _(n):
            feats = pl.ds(pl.multiple_of(n * 512, 512), 512)
            contract = (((1,), (1,)), ((), ()))
            out = lax.dot_general(gs[1, rows, :], wg[feats, :], contract, preferred_element_type=F32)
            out = out + lax.dot_general(
                gs[2, rows, :], wu[feats, :], contract, preferred_element_type=F32
            )
            rt[rows, feats] = out.astype(BF)

        rt[rows, 0:GL] = jnp.where(ends, dgs[rows, :].astype(F32), rt[rows, 0:GL].astype(F32)).astype(BF)

    def give_back(j):
        return pltpu.make_async_remote_copy(
            src_ref=rt.at[block(j)],
            dst_ref=back.at[block(me)],
            send_sem=b_ss,
            recv_sem=b_rs,
            device_id=origin(j),
            device_id_type=MESH,
        )

    def return_blocks(start, count):
        @pl.loop(max(start // SLOT, 1), (start + count) // SLOT)
        def _(j):
            give_back(j).start()

    for n, (start, count) in enumerate(CHUNKS):
        first = max(start, SLOT)
        here = xs.at[:, pl.ds(first, start + count - first)]
        pltpu.make_async_copy(here, here, d_rs.at[n]).wait()
        if n == len(CHUNKS) - 1:
            return_blocks(0, CHUNKS[0][1])
            back[block(me), :] = rt[0:SLOT, :]
        expert(pl.ds(start, count), count)
        if n == 0:
            input_rows(pl.ds(start, count), count)

    def half_of(u):
        return jnp.where(u < 3, 1 - my_half, my_half)

    def tile(u, to_x, half):
        kind = u % 3
        start = (half_of(u) * 4 + (to_x + 4) % 4) * 256 + half * HALF
        left = xs[jnp.where(kind == 0, 1, 0), :, pl.ds(pl.multiple_of(start, HALF), HALF)]
        return lax.dot_general(
            left, gs[kind], (((0,), (0,)), ((), ())), preferred_element_type=F32
        )

    def message(u, m):
        step = 1 if m % 2 == 0 else -1
        return pltpu.make_async_remote_copy(
            src_ref=rs_s.at[u * MSGS + m],
            dst_ref=rs_r.at[u * MSGS + m],
            send_sem=r_ss,
            recv_sem=r_rs.at[u * MSGS + m],
            device_id=device(x + step, y, z, c),
            device_id_type=MESH,
        )

    def send(u, m, tile_value):
        rs_s[u * MSGS + m] = tile_value.astype(BF)
        message(u, m).start()

    def received(u, m):
        message(u, m).wait_recv()
        return rs_r[u * MSGS + m].astype(F32)

    def to_partner(n, half):
        return pltpu.make_async_remote_copy(
            src_ref=z_s.at[n * 2 + half],
            dst_ref=z_r.at[n * 2 + half],
            send_sem=z_ss,
            recv_sem=z_rs.at[n * 2 + half],
            device_id=device(x, y, z + 4, c),
            device_id_type=MESH,
        )

    def token_gradients():
        others = back.at[pl.ds(SLOT, ROWS - SLOT)]
        pltpu.make_async_copy(others, others, b_rs).wait()
        for n in range(D // 512):
            cols = pl.ds(n * 512, 512)
            dtok_ref[:, cols] = jnp.dot(sel[...], back[:, cols], preferred_element_type=F32).astype(BF)
        ends = iota((ROWS, GL), 0) % SLOT == SLOT - 1
        row = jnp.sum(jnp.where(ends, back[:, 0:GL].astype(F32), 0.0), axis=0, keepdims=True)
        picked = sel[...].astype(F32) * row
        at = iota((TOK, TOP), 1)
        named = ids_ref[...].T
        grads = jnp.zeros((TOK, TOP), F32)
        for k in range(TOP):
            hit = named[:, k : k + 1] == iota((TOK, GL), 1) // SLOT
            one = jnp.sum(jnp.where(hit, picked, 0.0), axis=1, keepdims=True)
            grads = jnp.where(at == k, one, grads)
        dgate_ref[...] = grads.T.astype(BF)

    def finish(n):
        ref = (owd_ref, owg_ref, owu_ref)[n]
        for half in range(2):
            to_partner(n, half).wait_recv()
            total = own[n * 2 + half] + z_r[n * 2 + half].astype(F32)
            if n == 0:
                ref[0, :, half * HALF : (half + 1) * HALF] = total.T.astype(BF)
            else:
                ref[0, half * HALF : (half + 1) * HALF, :] = total.astype(BF)

    @pl.loop(0, UNITS + 2)
    def _(v):
        @pl.when(v < UNITS)
        def _():
            u = v
            send(u, 0, tile(u, x + 2, 0))
            send(u, 1, tile(u, x + 2, 1))
            send(u, 2, tile(u, x + 1, 1))
            send(u, 3, tile(u, x - 1, 0))

        @pl.when(v == 1)
        def _():
            start = CHUNKS[1][0]
            input_rows(pl.ds(start, ROWS - start), ROWS - start)
            return_blocks(start, ROWS - start)

        @pl.when(v == UNITS)
        def _():
            token_gradients()
            finish(0)

        @pl.when(v == UNITS + 1)
        def _():
            finish(1)

        @pl.when((v >= 1) & (v < UNITS + 1))
        def _():
            u = v - 1
            send(u, 4, tile(u, x + 1, 0) + received(u, 0))
            send(u, 5, tile(u, x - 1, 1) + received(u, 1))

        @pl.when(v >= 2)
        def _():
            u = v - 2
            for half in range(2):
                total = tile(u, x, half) + received(u, 4 + half) + received(u, 3 - half)

                @pl.when(u < 3)
                def _():
                    z_s[u * 2 + half] = total.astype(BF)
                    to_partner(u, half).start()

                @pl.when(u >= 3)
                def _():
                    own[(u - 3) * 2 + half] = total

    finish(2)

    rest = pl.ds(SLOT, ROWS - SLOT)
    for ref, sem in (
        (xs.at[:, rest], d_ss), (relay, h_ss), (rt.at[rest], b_ss), (rs_s, r_ss), (z_s, z_ss),
    ):
        pltpu.make_async_remote_copy(
            src_ref=ref, dst_ref=ref, send_sem=sem, recv_sem=sem,
            device_id=device(x + 1, y, z, c), device_id_type=MESH,
        ).wait_send()


def settle(*refs):
    ins, outs, sem = refs[:5], refs[5:10], refs[10]
    puts = [pltpu.make_async_copy(ins[i], outs[i], sem.at[i]) for i in range(5)]
    for put in puts:
        put.start()
    for put in puts:
        put.wait()


def body(tokens, out_grad, expert_ids, gate_vals, w_gate, w_up, w_down):
    vmem = pl.BlockSpec(memory_space=pltpu.VMEM)
    hbm = pl.BlockSpec(memory_space=pl.ANY)
    dma = pltpu.SemaphoreType.DMA
    shapes = (
        jax.ShapeDtypeStruct((TOK, D), BF),
        jax.ShapeDtypeStruct((TOP, TOK), BF),
        jax.ShapeDtypeStruct((1, 256, FF), BF),
        jax.ShapeDtypeStruct((1, 256, FF), BF),
        jax.ShapeDtypeStruct((1, FF, 256), BF),
    )
    outs = pl.pallas_call(
        kernel,
        out_shape=shapes,
        in_specs=[pl.BlockSpec(memory_space=pltpu.HBM)] * 2 + [hbm] * 5,
        out_specs=[vmem] * 5,
        scratch_shapes=[
            pltpu.VMEM((TOP, TOK), jnp.int32),
            pltpu.VMEM((TOP, TOK), BF),
            pltpu.VMEM((TOK, D), BF),
            pltpu.VMEM((TOK, D), BF),
            pltpu.VMEM((D, FF), BF),
            pltpu.VMEM((D, FF), BF),
            pltpu.VMEM((FF, D), BF),
            pltpu.VMEM((2, ROWS, D), BF),
            pltpu.VMEM((2, RELAYS * SLOT, D), BF),
            pltpu.VMEM((2, ROWS, D), BF),
            pltpu.VMEM((TOK, GL), BF),
            pltpu.VMEM((3, ROWS, FF), BF),
            pltpu.VMEM((ROWS, D), BF),
            pltpu.VMEM((ROWS, D), BF),
            pltpu.VMEM((ROWS, GL), BF),
            pltpu.VMEM((UNITS * MSGS, HALF, FF), BF),
            pltpu.VMEM((UNITS * MSGS, HALF, FF), BF),
            pltpu.VMEM((6, HALF, FF), F32),
            pltpu.VMEM((6, HALF, FF), BF),
            pltpu.VMEM((6, HALF, FF), BF),
            dma((7,)),
            dma,
            dma((2, RELAYS)),
            dma,
            dma((3,)),
            dma,
            dma,
            dma,
            dma((UNITS * MSGS,)),
            dma,
            dma((6,)),
        ],
        compiler_params=pltpu.CompilerParams(
            collective_id=0, has_side_effects=True, vmem_limit_bytes=52 * 2**20
        ),
    )(pltpu.with_memory_space_constraint(expert_ids.T, pltpu.HBM), pltpu.with_memory_space_constraint(gate_vals.T, pltpu.HBM), tokens, out_grad, w_gate, w_up, w_down)
    d_tokens, d_gates, d_gate, d_up, d_down = pl.pallas_call(
        settle,
        out_shape=shapes,
        in_specs=[hbm] * 5,
        out_specs=[hbm] * 5,
        scratch_shapes=[dma((5,))],
        compiler_params=pltpu.CompilerParams(vmem_limit_bytes=2**20),
    )(*outs)
    return d_tokens, d_gates.T, d_gate, d_up, d_down


def solution(mesh):
    in_specs = (
        P(("dp", "expert"), None),
        P(("dp", "expert"), None),
        P(("dp", "expert"), None),
        P(("dp", "expert"), None),
        P("expert", None, None),
        P("expert", None, None),
        P("expert", None, None),
    )
    out_specs = (
        P(("dp", "expert"), None),
        P(("dp", "expert"), None),
        P("expert", "dp", None),
        P("expert", "dp", None),
        P("expert", None, "dp"),
    )
    return jax.shard_map(body, mesh=mesh, in_specs=in_specs, out_specs=out_specs, check_vma=False)
```

```python
import functools

import jax
import jax.numpy as jnp
from jax import lax
from jax.experimental import pallas as pl
from jax.experimental.pallas import tpu as pltpu
from jax.sharding import PartitionSpec as P

MESH = pl.DeviceIdType.MESH
BF = jnp.bfloat16
F32 = jnp.float32

TOK = 160
TOP = 8
D = 2048
FF = 768
NE = 32
SLOT = 16
ROWS = NE * SLOT
GL = NE * SLOT
UNITS = 6
MSGS = 6
HALF = 128
FIRST = 14
RELAYS = NE - FIRST
WIDTH = (D - 128, D)
CHUNKS = ((0, 224), (224, 144), (368, 144))
LAST = CHUNKS[2][0] // SLOT


def coords():
    dp, ex = lax.axis_index("dp"), lax.axis_index("expert")
    return dp % 4, ex // 8, (dp // 4) * 4 + (ex // 2) % 4, ex % 2


def device(x, y, z, c):
    z = (z + 8) % 8
    return {"dp": (z // 4) * 4 + (x + 4) % 4, "expert": (((y + 4) % 4) * 4 + z % 4) * 2 + c}


def offset(j):
    q, r = j // 2, (j - FIRST) // 2
    plain = j < FIRST
    dy = jnp.where(plain, jnp.where(q < 4, q, 0), 1 + r % 3)
    kind = jnp.where(plain, jnp.where(q < 4, 0, q - 3), 1 + (r % 3 + r // 3) % 3)
    return dy, kind, j % 2


def z_shift(kind, core):
    return jnp.where(kind == 1, 1, 0) - jnp.where(kind == 2, 1, 0) + jnp.where(kind == 3, 2 - 4 * core, 0)


def target(j):
    x, y, z, c = coords()
    dy, kind, dc = offset(j)
    return device(x, y + dy, z + z_shift(kind, c), (c + dc) % 2)


def origin(j):
    x, y, z, c = coords()
    dy, kind, dc = offset(j)
    c0 = (c + dc) % 2
    return device(x, y - dy, z - z_shift(kind, c0), c0)


def target_expert(j):
    x, y, z, c = coords()
    dy, kind, dc = offset(j)
    return (((y + dy) % 4) * 4 + (z + z_shift(kind, c) + 8) % 4) * 2 + (c + dc) % 2


def turn(j, p, second):
    x, y, z, c = coords()
    dy, kind, dc = offset(j)
    if second == (p == 0):
        return device(x, y + dy, z, c)
    return device(x, y, z + z_shift(kind, c), (c + dc) % 2)


def peers():
    x, y, z, c = coords()
    for dz in (0, 1, -1, 2, -2):
        for dy in range(4):
            for dc in (0, 1):
                if (dz, dy, dc) != (0, 0, 0):
                    yield device(x, y + dy, z + dz, (c + dc) % 2)
    yield device(x + 1, y, z, c)
    yield device(x - 1, y, z, c)
    yield device(x, y, z + 4, c)


def block(j):
    return pl.ds(pl.multiple_of(j * SLOT, SLOT), SLOT)


def iota(shape, dim):
    return lax.broadcasted_iota(jnp.int32, shape, dim)


def kernel(
    ids_hbm, gate_hbm, tok_hbm, dy_hbm, wg_hbm, wu_hbm, wd_hbm,
    dtok_ref, dgate_ref, owg_ref, owu_ref, owd_ref,
    ids_ref, gate_ref, tok_ref, dy_ref, wg, wu, wd, sent, relay, xs, sel, gs, rt, back, dgs, rs_s, rs_r, own, z_s, z_r,
    w_sem, h_ss, h_rs, d_ss, d_rs, b_ss, b_rs, r_ss, r_rs, z_ss, z_rs,
):
    x, y, z, c = coords()
    me = lax.axis_index("expert")
    my_half = lax.axis_index("dp") // 4

    barrier = pltpu.get_barrier_semaphore()
    count = 0
    for peer in peers():
        pl.semaphore_signal(barrier, inc=1, device_id=peer, device_id_type=MESH)
        count += 1

    loads = [
        pltpu.make_async_copy(src, dst, w_sem.at[n])
        for n, (src, dst) in enumerate(
            ((ids_hbm, ids_ref), (gate_hbm, gate_ref), (tok_hbm, tok_ref), (dy_hbm, dy_ref), (wg_hbm.at[0], wg), (wu_hbm.at[0], wu), (wd_hbm.at[0], wd))
        )
    ]
    for load in loads:
        load.start()

    expert_of = iota((TOK, GL), 1) // SLOT
    loads[0].wait()
    loads[1].wait()
    ids = ids_ref[...].T
    gates = gate_ref[...].astype(F32).T
    member = jnp.zeros((TOK, GL), F32)
    value = jnp.zeros((TOK, GL), F32)
    for k in range(TOP):
        hit = ids[:, k : k + 1] == expert_of
        member = jnp.where(hit, 1.0, member)
        value = jnp.where(hit, gates[:, k : k + 1], value)
    earlier = (iota((TOK, TOK), 1) < iota((TOK, TOK), 0)).astype(F32).astype(BF)
    rank = jnp.dot(earlier, member.astype(BF), preferred_element_type=F32)
    slot_of = (iota((TOK, GL), 1) % SLOT).astype(F32)
    chosen = jnp.where(rank == slot_of, member, 0.0)
    sel[...] = chosen.astype(BF)
    gate_row = jnp.sum(chosen * value, axis=0, keepdims=True)
    pick = chosen.T.astype(BF)
    at_end = iota((NE, SLOT, 128), 1) == SLOT - 1
    loads[2].wait()
    tail = jnp.dot(pick, tok_ref[:, WIDTH[0] :], preferred_element_type=F32).reshape(NE, SLOT, 128)
    for n in range(4):
        first, stop = n * 512, min(n * 512 + 512, WIDTH[0])
        rows = jnp.dot(pick, tok_ref[:, first:stop], preferred_element_type=F32)
        for k in range(0, stop - first, 128):
            r = (first + k) // 128
            part = rows[:, k : k + 128].reshape(NE, SLOT, 128)
            part = jnp.where(at_end, tail[:, r : r + 1, :], part)
            sent[0, :, first + k : first + k + 128] = part.reshape(ROWS, 128).astype(BF)

    pl.semaphore_wait(barrier, count)

    def arrival(p, j, src, to):
        return pltpu.make_async_remote_copy(
            src_ref=src,
            dst_ref=xs.at[p, block(j), 0 : WIDTH[p]],
            send_sem=d_ss.at[p],
            recv_sem=d_rs.at[p, jnp.where(j < FIRST, 0, jnp.where(j < LAST, 1, 2))],
            device_id=to,
            device_id_type=MESH,
        )

    def direct(p, j):
        return arrival(p, j, sent.at[p, block(target_expert(j)), 0 : WIDTH[p]], target(j))

    def hop(p, r):
        j = r + FIRST
        return pltpu.make_async_remote_copy(
            src_ref=sent.at[p, block(target_expert(j)), 0 : WIDTH[p]],
            dst_ref=relay.at[p, block(r), 0 : WIDTH[p]],
            send_sem=h_ss.at[p],
            recv_sem=h_rs.at[p, r],
            device_id=turn(j, p, False),
            device_id_type=MESH,
        )

    def onward(p, r):
        j = r + FIRST
        return arrival(p, j, relay.at[p, block(r), 0 : WIDTH[p]], turn(j, p, True))

    @pl.loop(0, RELAYS)
    def _(r):
        hop(0, r).start()

    @pl.loop(1, FIRST)
    def _(j):
        direct(0, j).start()

    last = iota((ROWS, 512), 0) % SLOT == SLOT - 1
    loads[3].wait()
    for n in range(D // 512):
        cols = pl.ds(n * 512, 512)
        rows = jnp.dot(pick, dy_ref[:, cols], preferred_element_type=F32)
        if n == 0:
            rows = jnp.where(last, gate_row, rows)
        sent[1, :, cols] = rows.astype(BF)

    @pl.loop(0, RELAYS)
    def _(r):
        hop(1, r).start()

    @pl.loop(1, FIRST)
    def _(j):
        direct(1, j).start()

    for p in range(2):
        xs[p, 0:SLOT, 0 : WIDTH[p]] = sent[p, block(me), 0 : WIDTH[p]]
    for load in loads[4:]:
        load.wait()

    @pl.loop(0, RELAYS)
    def _(r):
        for p in range(2):
            hop(p, r).wait_recv()
            onward(p, r).start()

    lane = iota((1, SLOT, GL), 2)
    mine = lane == me * SLOT + iota((1, SLOT, GL), 1)

    def expert(rows, count):
        place = iota((1, SLOT, 128), 1)
        tail = jnp.zeros((count // SLOT, SLOT, 128), F32)
        for r in range(SLOT - 1):
            part = xs[0, rows, r * 128 : (r + 1) * 128].astype(F32).reshape(count // SLOT, SLOT, 128)
            tail = jnp.where(place == r, part[:, SLOT - 1 : SLOT, :], tail)
        xs[0, rows, WIDTH[0] :] = tail.reshape(count, 128).astype(BF)
        row = xs[1, rows, 0:GL].astype(F32).reshape(count // SLOT, SLOT, GL)
        row = jnp.where(iota((1, SLOT, GL), 1) == SLOT - 1, row, 0.0)
        row = jnp.sum(row, axis=1, keepdims=True)
        scale = jnp.sum(jnp.where(mine, row, 0.0), axis=2, keepdims=True).reshape(count, 1)

        def part(f, total):
            cols = pl.ds(pl.multiple_of(f * 256, 256), 256)
            gate_pre = jnp.dot(xs[0, rows, :], wg[:, cols], preferred_element_type=F32)
            up_pre = jnp.dot(xs[0, rows, :], wu[:, cols], preferred_element_type=F32)
            raw = lax.dot_general(
                xs[1, rows, :], wd[cols, :], (((1,), (1,)), ((), ())), preferred_element_type=F32
            )
            sig = jax.nn.sigmoid(gate_pre)
            silu = gate_pre * sig
            hidden = (silu * up_pre).astype(BF)
            grad = scale * raw
            gs[2, rows, cols] = (grad * silu).astype(BF)
            gs[1, rows, cols] = (grad * up_pre * sig * (1.0 + gate_pre * (1.0 - sig))).astype(BF)
            gs[0, rows, cols] = hidden
            return total + jnp.sum(hidden.astype(F32) * raw, axis=1, keepdims=True)

        total = lax.fori_loop(0, FF // 256, part, jnp.zeros((count, 1), F32))
        grads = total.astype(BF).astype(F32).reshape(count // SLOT, SLOT, 1)
        grads = jnp.sum(jnp.where(mine, grads, 0.0), axis=1, keepdims=True)
        grads = jnp.broadcast_to(grads, (count // SLOT, SLOT, GL)).reshape(count, GL)
        dgs[rows, :] = grads.astype(BF)
        xs[1, rows, :] = (scale * xs[1, rows, :].astype(F32)).astype(BF)

    def input_rows(rows, count):
        ends = iota((count, GL), 0) % SLOT == SLOT - 1

        @pl.loop(0, D // 512)
        def _(n):
            feats = pl.ds(pl.multiple_of(n * 512, 512), 512)
            contract = (((1,), (1,)), ((), ()))
            out = lax.dot_general(gs[1, rows, :], wg[feats, :], contract, preferred_element_type=F32)
            out = out + lax.dot_general(
                gs[2, rows, :], wu[feats, :], contract, preferred_element_type=F32
            )
            rt[rows, feats] = out.astype(BF)

        rt[rows, 0:GL] = jnp.where(ends, dgs[rows, :].astype(F32), rt[rows, 0:GL].astype(F32)).astype(BF)

    def give_back(j):
        return pltpu.make_async_remote_copy(
            src_ref=rt.at[block(j)],
            dst_ref=back.at[block(me)],
            send_sem=b_ss,
            recv_sem=b_rs,
            device_id=origin(j),
            device_id_type=MESH,
        )

    def return_blocks(start, count):
        @pl.loop(max(start // SLOT, 1), (start + count) // SLOT)
        def _(j):
            give_back(j).start()

    for n, (start, count) in enumerate(CHUNKS):
        first = max(start, SLOT)
        for p in range(2):
            here = xs.at[p, pl.ds(first, start + count - first), 0 : WIDTH[p]]
            pltpu.make_async_copy(here, here, d_rs.at[p, n]).wait()
        if n == len(CHUNKS) - 1:
            return_blocks(0, start)
            back[block(me), :] = rt[0:SLOT, :]
        expert(pl.ds(start, count), count)
        if n < 2:
            input_rows(pl.ds(start, count), count)

    def half_of(u):
        return jnp.where(u < 3, 1 - my_half, my_half)

    def tile(u, to_x, half):
        kind = u % 3
        start = (half_of(u) * 4 + (to_x + 4) % 4) * 256 + half * HALF
        left = xs[jnp.where(kind == 0, 1, 0), :, pl.ds(pl.multiple_of(start, HALF), HALF)]
        return lax.dot_general(
            left, gs[kind], (((0,), (0,)), ((), ())), preferred_element_type=F32
        )

    def message(u, m):
        step = 1 if m % 2 == 0 else -1
        return pltpu.make_async_remote_copy(
            src_ref=rs_s.at[u * MSGS + m],
            dst_ref=rs_r.at[u * MSGS + m],
            send_sem=r_ss,
            recv_sem=r_rs.at[u * MSGS + m],
            device_id=device(x + step, y, z, c),
            device_id_type=MESH,
        )

    def send(u, m, tile_value):
        rs_s[u * MSGS + m] = tile_value.astype(BF)
        message(u, m).start()

    def received(u, m):
        message(u, m).wait_recv()
        return rs_r[u * MSGS + m].astype(F32)

    def to_partner(n, half):
        return pltpu.make_async_remote_copy(
            src_ref=z_s.at[n * 2 + half],
            dst_ref=z_r.at[n * 2 + half],
            send_sem=z_ss,
            recv_sem=z_rs.at[n * 2 + half],
            device_id=device(x, y, z + 4, c),
            device_id_type=MESH,
        )

    def token_gradients():
        others = back.at[pl.ds(SLOT, ROWS - SLOT)]
        pltpu.make_async_copy(others, others, b_rs).wait()
        for n in range(D // 512):
            cols = pl.ds(n * 512, 512)
            dtok_ref[:, cols] = jnp.dot(sel[...], back[:, cols], preferred_element_type=F32).astype(BF)
        ends = iota((ROWS, GL), 0) % SLOT == SLOT - 1
        row = jnp.sum(jnp.where(ends, back[:, 0:GL].astype(F32), 0.0), axis=0, keepdims=True)
        picked = sel[...].astype(F32) * row
        at = iota((TOK, TOP), 1)
        named = ids_ref[...].T
        grads = jnp.zeros((TOK, TOP), F32)
        for k in range(TOP):
            hit = named[:, k : k + 1] == iota((TOK, GL), 1) // SLOT
            one = jnp.sum(jnp.where(hit, picked, 0.0), axis=1, keepdims=True)
            grads = jnp.where(at == k, one, grads)
        dgate_ref[...] = grads.T.astype(BF)

    def finish(n):
        ref = (owd_ref, owg_ref, owu_ref)[n]
        for half in range(2):
            to_partner(n, half).wait_recv()
            total = own[n * 2 + half] + z_r[n * 2 + half].astype(F32)
            if n == 0:
                ref[0, :, half * HALF : (half + 1) * HALF] = total.T.astype(BF)
            else:
                ref[0, half * HALF : (half + 1) * HALF, :] = total.astype(BF)

    @pl.loop(0, UNITS + 2)
    def _(v):
        @pl.when(v < UNITS)
        def _():
            u = v
            send(u, 0, tile(u, x + 2, 0))
            send(u, 1, tile(u, x + 2, 1))

        @pl.when(v == 1)
        def _():
            start = CHUNKS[2][0]
            input_rows(pl.ds(start, ROWS - start), ROWS - start)
            return_blocks(start, ROWS - start)

        @pl.when(v == UNITS)
        def _():
            token_gradients()
            finish(0)

        @pl.when(v == UNITS + 1)
        def _():
            finish(1)

        @pl.when((v >= 1) & (v < UNITS + 1))
        def _():
            u = v - 1
            send(u, 4, tile(u, x + 1, 0) + received(u, 0))
            send(u, 5, tile(u, x - 1, 1) + received(u, 1))

        @pl.when(v < UNITS)
        def _():
            u = v
            send(u, 2, tile(u, x + 1, 1))
            send(u, 3, tile(u, x - 1, 0))

        @pl.when(v >= 2)
        def _():
            u = v - 2
            for half in range(2):
                total = tile(u, x, half) + received(u, 4 + half) + received(u, 3 - half)

                @pl.when(u < 3)
                def _():
                    z_s[u * 2 + half] = total.astype(BF)
                    to_partner(u, half).start()

                @pl.when(u >= 3)
                def _():
                    own[(u - 3) * 2 + half] = total

    finish(2)

    rest = pl.ds(SLOT, ROWS - SLOT)
    for ref, sem in (
        (xs.at[0, rest, 0 : WIDTH[0]], d_ss.at[0]), (xs.at[1, rest], d_ss.at[1]),
        (relay.at[0, :, 0 : WIDTH[0]], h_ss.at[0]), (relay.at[1], h_ss.at[1]), (rt.at[rest], b_ss), (rs_s, r_ss), (z_s, z_ss),
    ):
        pltpu.make_async_remote_copy(
            src_ref=ref, dst_ref=ref, send_sem=sem, recv_sem=sem,
            device_id=device(x + 1, y, z, c), device_id_type=MESH,
        ).wait_send()


def settle(*refs):
    ins, outs, sem = refs[:5], refs[5:10], refs[10]
    puts = [pltpu.make_async_copy(ins[i], outs[i], sem.at[i]) for i in range(5)]
    for put in puts:
        put.start()
    for put in puts:
        put.wait()


def body(tokens, out_grad, expert_ids, gate_vals, w_gate, w_up, w_down):
    vmem = pl.BlockSpec(memory_space=pltpu.VMEM)
    hbm = pl.BlockSpec(memory_space=pl.ANY)
    dma = pltpu.SemaphoreType.DMA
    shapes = (
        jax.ShapeDtypeStruct((TOK, D), BF),
        jax.ShapeDtypeStruct((TOP, TOK), BF),
        jax.ShapeDtypeStruct((1, 256, FF), BF),
        jax.ShapeDtypeStruct((1, 256, FF), BF),
        jax.ShapeDtypeStruct((1, FF, 256), BF),
    )
    outs = pl.pallas_call(
        kernel,
        out_shape=shapes,
        in_specs=[pl.BlockSpec(memory_space=pltpu.HBM)] * 2 + [hbm] * 5,
        out_specs=[vmem] * 5,
        scratch_shapes=[
            pltpu.VMEM((TOP, TOK), jnp.int32),
            pltpu.VMEM((TOP, TOK), BF),
            pltpu.VMEM((TOK, D), BF),
            pltpu.VMEM((TOK, D), BF),
            pltpu.VMEM((D, FF), BF),
            pltpu.VMEM((D, FF), BF),
            pltpu.VMEM((FF, D), BF),
            pltpu.VMEM((2, ROWS, D), BF),
            pltpu.VMEM((2, RELAYS * SLOT, D), BF),
            pltpu.VMEM((2, ROWS, D), BF),
            pltpu.VMEM((TOK, GL), BF),
            pltpu.VMEM((3, ROWS, FF), BF),
            pltpu.VMEM((ROWS, D), BF),
            pltpu.VMEM((ROWS, D), BF),
            pltpu.VMEM((ROWS, GL), BF),
            pltpu.VMEM((UNITS * MSGS, HALF, FF), BF),
            pltpu.VMEM((UNITS * MSGS, HALF, FF), BF),
            pltpu.VMEM((6, HALF, FF), F32),
            pltpu.VMEM((6, HALF, FF), BF),
            pltpu.VMEM((6, HALF, FF), BF),
            dma((7,)),
            dma((2,)),
            dma((2, RELAYS)),
            dma((2,)),
            dma((2, 3)),
            dma,
            dma,
            dma,
            dma((UNITS * MSGS,)),
            dma,
            dma((6,)),
        ],
        compiler_params=pltpu.CompilerParams(
            collective_id=0, has_side_effects=True, vmem_limit_bytes=52 * 2**20
        ),
    )(pltpu.with_memory_space_constraint(expert_ids.T, pltpu.HBM), pltpu.with_memory_space_constraint(gate_vals.T, pltpu.HBM), tokens, out_grad, w_gate, w_up, w_down)
    d_tokens, d_gates, d_gate, d_up, d_down = pl.pallas_call(
        settle,
        out_shape=shapes,
        in_specs=[hbm] * 5,
        out_specs=[hbm] * 5,
        scratch_shapes=[dma((5,))],
        compiler_params=pltpu.CompilerParams(vmem_limit_bytes=2**20),
    )(*outs)
    return d_tokens, d_gates.T, d_gate, d_up, d_down


def solution(mesh):
    in_specs = (
        P(("dp", "expert"), None),
        P(("dp", "expert"), None),
        P(("dp", "expert"), None),
        P(("dp", "expert"), None),
        P("expert", None, None),
        P("expert", None, None),
        P("expert", None, None),
    )
    out_specs = (
        P(("dp", "expert"), None),
        P(("dp", "expert"), None),
        P("expert", "dp", None),
        P("expert", "dp", None),
        P("expert", None, "dp"),
    )
    return jax.shard_map(body, mesh=mesh, in_specs=in_specs, out_specs=out_specs, check_vma=False)
```

```python
import functools

import jax
import jax.numpy as jnp
from jax import lax
from jax.experimental import pallas as pl
from jax.experimental.pallas import tpu as pltpu
from jax.sharding import PartitionSpec as P

MESH = pl.DeviceIdType.MESH
BF = jnp.bfloat16
F32 = jnp.float32

TOK = 160
TOP = 8
D = 2048
FF = 768
NE = 32
SLOT = 16
ROWS = NE * SLOT
GL = NE * SLOT
UNITS = 6
MSGS = 6
HALF = 128
FIRST = 14
RELAYS = NE - FIRST
WIDTH = D - 128
CHUNKS = ((0, 224), (224, 144), (368, 144))
LAST = CHUNKS[2][0] // SLOT


def coords():
    dp, ex = lax.axis_index("dp"), lax.axis_index("expert")
    return dp % 4, ex // 8, (dp // 4) * 4 + (ex // 2) % 4, ex % 2


def device(x, y, z, c):
    z = (z + 8) % 8
    return {"dp": (z // 4) * 4 + (x + 4) % 4, "expert": (((y + 4) % 4) * 4 + z % 4) * 2 + c}


def offset(j):
    q, r = j // 2, (j - FIRST) // 2
    plain = j < FIRST
    dy = jnp.where(plain, jnp.where(q < 4, q, 0), 1 + r % 3)
    kind = jnp.where(plain, jnp.where(q < 4, 0, q - 3), 1 + (r % 3 + r // 3) % 3)
    return dy, kind, j % 2


def z_shift(kind, core):
    return jnp.where(kind == 1, 1, 0) - jnp.where(kind == 2, 1, 0) + jnp.where(kind == 3, 2 - 4 * core, 0)


def target(j):
    x, y, z, c = coords()
    dy, kind, dc = offset(j)
    return device(x, y + dy, z + z_shift(kind, c), (c + dc) % 2)


def origin(j):
    x, y, z, c = coords()
    dy, kind, dc = offset(j)
    c0 = (c + dc) % 2
    return device(x, y - dy, z - z_shift(kind, c0), c0)


def target_expert(j):
    x, y, z, c = coords()
    dy, kind, dc = offset(j)
    return (((y + dy) % 4) * 4 + (z + z_shift(kind, c) + 8) % 4) * 2 + (c + dc) % 2


def turn(j, p, second):
    x, y, z, c = coords()
    dy, kind, dc = offset(j)
    if second == (p == 0):
        return device(x, y + dy, z, c)
    return device(x, y, z + z_shift(kind, c), (c + dc) % 2)


def peers():
    x, y, z, c = coords()
    for dz in (2, -2, 1, -1, 0):
        for dy in (2, 1, 3, 0):
            for dc in (0, 1):
                if (dz, dy, dc) != (0, 0, 0):
                    yield device(x, y + dy, z + dz, (c + dc) % 2)
    yield device(x + 1, y, z, c)
    yield device(x - 1, y, z, c)
    yield device(x, y, z + 4, c)


def block(j):
    return pl.ds(pl.multiple_of(j * SLOT, SLOT), SLOT)


def iota(shape, dim):
    return lax.broadcasted_iota(jnp.int32, shape, dim)


def kernel(
    ids_hbm, gate_hbm, tok_hbm, dy_hbm, wg_hbm, wu_hbm, wd_hbm,
    dtok_ref, dgate_ref, owg_ref, owu_ref, owd_ref,
    ids_ref, gate_ref, tok_ref, dy_ref, wg, wu, wd, pre, sent, relay, xs, sel, gs, rt, back, dgs, rs_s, rs_r, own, z_s, z_r,
    w_sem, h_ss, h_rs, d_ss, d_rs, b_ss, b_rs, r_ss, r_rs, z_ss, z_rs,
):
    x, y, z, c = coords()
    me = lax.axis_index("expert")
    my_half = lax.axis_index("dp") // 4

    barrier = pltpu.get_barrier_semaphore()
    count = 0
    for peer in peers():
        pl.semaphore_signal(barrier, inc=1, device_id=peer, device_id_type=MESH)
        count += 1

    loads = [
        pltpu.make_async_copy(src, dst, w_sem.at[n])
        for n, (src, dst) in enumerate(
            ((ids_hbm, ids_ref), (gate_hbm, gate_ref), (tok_hbm, tok_ref), (dy_hbm, dy_ref), (wg_hbm.at[0], wg), (wu_hbm.at[0], wu), (wd_hbm.at[0], wd))
        )
    ]
    for load in loads:
        load.start()

    expert_of = iota((TOK, GL), 1) // SLOT
    loads[0].wait()
    loads[1].wait()
    ids = ids_ref[...].T
    gates = gate_ref[...].astype(F32).T
    member = jnp.zeros((TOK, GL), F32)
    value = jnp.zeros((TOK, GL), F32)
    for k in range(TOP):
        hit = ids[:, k : k + 1] == expert_of
        member = jnp.where(hit, 1.0, member)
        value = jnp.where(hit, gates[:, k : k + 1], value)
    earlier = (iota((TOK, TOK), 1) < iota((TOK, TOK), 0)).astype(F32).astype(BF)
    rank = jnp.dot(earlier, member.astype(BF), preferred_element_type=F32)
    slot_of = (iota((TOK, GL), 1) % SLOT).astype(F32)
    chosen = jnp.where(rank == slot_of, member, 0.0)
    sel[...] = chosen.astype(BF)
    picks = chosen.T.astype(BF), (chosen * value).T.astype(BF)
    at_end = iota((NE, SLOT, 128), 1) == SLOT - 1

    def pack(p, ref):
        tail = jnp.dot(picks[p], ref[:, WIDTH:], preferred_element_type=F32).reshape(NE, SLOT, 128)
        for n in range(4):
            first, stop = n * 512, min(n * 512 + 512, WIDTH)
            rows = jnp.dot(picks[p], ref[:, first:stop], preferred_element_type=F32)
            for k in range(0, stop - first, 128):
                r = (first + k) // 128
                part = rows[:, k : k + 128].reshape(NE, SLOT, 128)
                part = jnp.where(at_end, tail[:, r : r + 1, :], part)
                sent[p, :, first + k : first + k + 128] = part.reshape(ROWS, 128).astype(BF)

    loads[2].wait()
    pack(0, tok_ref)

    pl.semaphore_wait(barrier, count)

    def arrival(p, j, src, to):
        return pltpu.make_async_remote_copy(
            src_ref=src,
            dst_ref=xs.at[p, block(j), 0 : WIDTH],
            send_sem=d_ss.at[p],
            recv_sem=d_rs.at[p, jnp.where(j < FIRST, 0, jnp.where(j < LAST, 1, 2))],
            device_id=to,
            device_id_type=MESH,
        )

    def direct(p, j):
        return arrival(p, j, sent.at[p, block(target_expert(j)), 0 : WIDTH], target(j))

    def hop(p, r):
        j = r + FIRST
        return pltpu.make_async_remote_copy(
            src_ref=sent.at[p, block(target_expert(j)), 0 : WIDTH],
            dst_ref=relay.at[p, block(r), 0 : WIDTH],
            send_sem=h_ss.at[p],
            recv_sem=h_rs.at[p, r],
            device_id=turn(j, p, False),
            device_id_type=MESH,
        )

    def onward(p, r):
        j = r + FIRST
        return arrival(p, j, relay.at[p, block(r), 0 : WIDTH], turn(j, p, True))

    @pl.loop(0, RELAYS)
    def _(r):
        hop(0, r).start()

    @pl.loop(1, FIRST)
    def _(j):
        direct(0, j).start()

    loads[3].wait()
    pack(1, dy_ref)

    @pl.loop(0, RELAYS)
    def _(r):
        hop(1, r).start()

    @pl.loop(1, FIRST)
    def _(j):
        direct(1, j).start()

    for p in range(2):
        xs[p, 0:SLOT, 0 : WIDTH] = sent[p, block(me), 0 : WIDTH]
    for load in loads[4:]:
        load.wait()

    @pl.loop(0, RELAYS)
    def _(r):
        for p in range(2):
            hop(p, r).wait_recv()
            onward(p, r).start()

    lane = iota((1, SLOT, GL), 2)
    mine = lane == me * SLOT + iota((1, SLOT, GL), 1)

    def live(count):
        return iota((count, 1), 0) % SLOT < SLOT - 1

    def forward(rows, count):
        place = iota((1, SLOT, 128), 1)
        for p in range(2):
            tail = jnp.zeros((count // SLOT, SLOT, 128), F32)
            for r in range(SLOT - 1):
                part = xs[p, rows, r * 128 : (r + 1) * 128].astype(F32)
                part = part.reshape(count // SLOT, SLOT, 128)
                tail = jnp.where(place == r, part[:, SLOT - 1 : SLOT, :], tail)
            xs[p, rows, WIDTH:] = tail.reshape(count, 128).astype(BF)

        @pl.loop(0, FF // 256)
        def _(f):
            cols = pl.ds(pl.multiple_of(f * 256, 256), 256)
            gate_pre = jnp.dot(xs[0, rows, :], wg[:, cols], preferred_element_type=F32)
            up_pre = jnp.dot(xs[0, rows, :], wu[:, cols], preferred_element_type=F32)
            pre[0, 0:count, cols] = gate_pre
            pre[1, 0:count, cols] = up_pre
            hidden = gate_pre * jax.nn.sigmoid(gate_pre) * up_pre
            gs[0, rows, cols] = jnp.where(live(count), hidden, 0.0).astype(BF)

    def backward(rows, count):
        def part(f, total):
            cols = pl.ds(pl.multiple_of(f * 256, 256), 256)
            grad = lax.dot_general(
                xs[1, rows, :], wd[cols, :], (((1,), (1,)), ((), ())), preferred_element_type=F32
            )
            grad = jnp.where(live(count), grad, 0.0)
            gate_pre, up_pre = pre[0, 0:count, cols], pre[1, 0:count, cols]
            sig = jax.nn.sigmoid(gate_pre)
            gs[2, rows, cols] = (grad * gate_pre * sig).astype(BF)
            gs[1, rows, cols] = (grad * up_pre * sig * (1.0 + gate_pre * (1.0 - sig))).astype(BF)
            return total + jnp.sum(gs[0, rows, cols].astype(F32) * grad, axis=1, keepdims=True)

        total = lax.fori_loop(0, FF // 256, part, jnp.zeros((count, 1), F32))
        grads = total.astype(BF).astype(F32).reshape(count // SLOT, SLOT, 1)
        grads = jnp.sum(jnp.where(mine, grads, 0.0), axis=1, keepdims=True)
        grads = jnp.broadcast_to(grads, (count // SLOT, SLOT, GL)).reshape(count, GL)
        dgs[rows, :] = grads.astype(BF)

    def input_rows(rows, count):
        ends = iota((count, GL), 0) % SLOT == SLOT - 1

        @pl.loop(0, D // 512)
        def _(n):
            feats = pl.ds(pl.multiple_of(n * 512, 512), 512)
            contract = (((1,), (1,)), ((), ()))
            out = lax.dot_general(gs[1, rows, :], wg[feats, :], contract, preferred_element_type=F32)
            out = out + lax.dot_general(
                gs[2, rows, :], wu[feats, :], contract, preferred_element_type=F32
            )
            rt[rows, feats] = out.astype(BF)

        rt[rows, 0:GL] = jnp.where(ends, dgs[rows, :].astype(F32), rt[rows, 0:GL].astype(F32)).astype(BF)

    def give_back(j):
        return pltpu.make_async_remote_copy(
            src_ref=rt.at[block(j)],
            dst_ref=back.at[block(me)],
            send_sem=b_ss,
            recv_sem=b_rs,
            device_id=origin(j),
            device_id_type=MESH,
        )

    def return_blocks(start, count):
        @pl.loop(max(start // SLOT, 1), (start + count) // SLOT)
        def _(j):
            give_back(j).start()

    for n, (start, count) in enumerate(CHUNKS):
        first = max(start, SLOT)
        for p in range(2):
            here = xs.at[p, pl.ds(first, start + count - first), 0 : WIDTH]
            pltpu.make_async_copy(here, here, d_rs.at[p, n]).wait()
        if n == len(CHUNKS) - 1:
            return_blocks(0, start)
            back[block(me), :] = rt[0:SLOT, :]
        forward(pl.ds(start, count), count)
        if n < 2:
            backward(pl.ds(start, count), count)
        if n < 2:
            input_rows(pl.ds(start, count), count)

    def half_of(u):
        return jnp.where(u < 3, 1 - my_half, my_half)

    def tile(u, to_x, half):
        kind = u % 3
        start = (half_of(u) * 4 + (to_x + 4) % 4) * 256 + half * HALF
        left = xs[jnp.where(kind == 0, 1, 0), :, pl.ds(pl.multiple_of(start, HALF), HALF)]
        return lax.dot_general(
            left, gs[kind], (((0,), (0,)), ((), ())), preferred_element_type=F32
        )

    def message(u, m):
        step = 1 if m % 2 == 0 else -1
        return pltpu.make_async_remote_copy(
            src_ref=rs_s.at[u * MSGS + m],
            dst_ref=rs_r.at[u * MSGS + m],
            send_sem=r_ss,
            recv_sem=r_rs.at[u * MSGS + m],
            device_id=device(x + step, y, z, c),
            device_id_type=MESH,
        )

    def send(u, m, tile_value):
        rs_s[u * MSGS + m] = tile_value.astype(BF)
        message(u, m).start()

    def received(u, m):
        message(u, m).wait_recv()
        return rs_r[u * MSGS + m].astype(F32)

    def to_partner(n, half):
        return pltpu.make_async_remote_copy(
            src_ref=z_s.at[n * 2 + half],
            dst_ref=z_r.at[n * 2 + half],
            send_sem=z_ss,
            recv_sem=z_rs.at[n * 2 + half],
            device_id=device(x, y, z + 4, c),
            device_id_type=MESH,
        )

    def token_gradients():
        others = back.at[pl.ds(SLOT, ROWS - SLOT)]
        pltpu.make_async_copy(others, others, b_rs).wait()
        for n in range(D // 512):
            cols = pl.ds(n * 512, 512)
            dtok_ref[:, cols] = jnp.dot(sel[...], back[:, cols], preferred_element_type=F32).astype(BF)
        ends = iota((ROWS, GL), 0) % SLOT == SLOT - 1
        row = jnp.sum(jnp.where(ends, back[:, 0:GL].astype(F32), 0.0), axis=0, keepdims=True)
        picked = sel[...].astype(F32) * row
        at = iota((TOK, TOP), 1)
        named = ids_ref[...].T
        weights = gate_ref[...].astype(F32).T
        grads = jnp.zeros((TOK, TOP), F32)
        for k in range(TOP):
            hit = named[:, k : k + 1] == iota((TOK, GL), 1) // SLOT
            one = jnp.sum(jnp.where(hit, picked, 0.0), axis=1, keepdims=True)
            grads = jnp.where(at == k, one, grads)
        dgate_ref[...] = (grads / weights).T.astype(BF)

    def finish(n):
        ref = (owd_ref, owg_ref, owu_ref)[n]
        for half in range(2):
            to_partner(n, half).wait_recv()
            total = own[n * 2 + half] + z_r[n * 2 + half].astype(F32)
            if n == 0:
                ref[0, :, half * HALF : (half + 1) * HALF] = total.T.astype(BF)
            else:
                ref[0, half * HALF : (half + 1) * HALF, :] = total.astype(BF)

    @pl.loop(0, UNITS + 2)
    def _(v):
        @pl.when(v < UNITS)
        def _():
            u = v
            send(u, 0, tile(u, x + 2, 0))
            send(u, 1, tile(u, x + 2, 1))

        @pl.when(v == 1)
        def _():
            start = CHUNKS[2][0]
            input_rows(pl.ds(start, ROWS - start), ROWS - start)
            return_blocks(start, ROWS - start)

        @pl.when(v == UNITS)
        def _():
            token_gradients()
            finish(0)

        @pl.when(v == UNITS + 1)
        def _():
            finish(1)

        @pl.when((v >= 1) & (v < UNITS + 1))
        def _():
            u = v - 1
            send(u, 4, tile(u, x + 1, 0) + received(u, 0))
            send(u, 5, tile(u, x - 1, 1) + received(u, 1))

        @pl.when(v < UNITS)
        def _():
            u = v
            send(u, 2, tile(u, x + 1, 1))
            send(u, 3, tile(u, x - 1, 0))

        @pl.when(v == 0)
        def _():
            backward(pl.ds(CHUNKS[2][0], CHUNKS[2][1]), CHUNKS[2][1])

        @pl.when(v >= 2)
        def _():
            u = v - 2
            for half in range(2):
                total = tile(u, x, half) + received(u, 4 + half) + received(u, 3 - half)

                @pl.when(u < 3)
                def _():
                    z_s[u * 2 + half] = total.astype(BF)
                    to_partner(u, half).start()

                @pl.when(u >= 3)
                def _():
                    own[(u - 3) * 2 + half] = total

    finish(2)

    rest = pl.ds(SLOT, ROWS - SLOT)
    for ref, sem in (
        (xs.at[0, rest, 0 : WIDTH], d_ss.at[0]), (xs.at[1, rest, 0:WIDTH], d_ss.at[1]),
        (relay.at[0, :, 0 : WIDTH], h_ss.at[0]), (relay.at[1, :, 0:WIDTH], h_ss.at[1]), (rt.at[rest], b_ss), (rs_s, r_ss), (z_s, z_ss),
    ):
        pltpu.make_async_remote_copy(
            src_ref=ref, dst_ref=ref, send_sem=sem, recv_sem=sem,
            device_id=device(x + 1, y, z, c), device_id_type=MESH,
        ).wait_send()


def settle(*refs):
    ins, outs, sem = refs[:5], refs[5:10], refs[10]
    puts = [pltpu.make_async_copy(ins[i], outs[i], sem.at[i]) for i in range(5)]
    for put in puts:
        put.start()
    for put in puts:
        put.wait()


def body(tokens, out_grad, expert_ids, gate_vals, w_gate, w_up, w_down):
    vmem = pl.BlockSpec(memory_space=pltpu.VMEM)
    hbm = pl.BlockSpec(memory_space=pl.ANY)
    dma = pltpu.SemaphoreType.DMA
    shapes = (
        jax.ShapeDtypeStruct((TOK, D), BF),
        jax.ShapeDtypeStruct((TOP, TOK), BF),
        jax.ShapeDtypeStruct((1, 256, FF), BF),
        jax.ShapeDtypeStruct((1, 256, FF), BF),
        jax.ShapeDtypeStruct((1, FF, 256), BF),
    )
    outs = pl.pallas_call(
        kernel,
        out_shape=shapes,
        in_specs=[pl.BlockSpec(memory_space=pltpu.HBM)] * 2 + [hbm] * 5,
        out_specs=[vmem] * 5,
        scratch_shapes=[
            pltpu.VMEM((TOP, TOK), jnp.int32),
            pltpu.VMEM((TOP, TOK), BF),
            pltpu.VMEM((TOK, D), BF),
            pltpu.VMEM((TOK, D), BF),
            pltpu.VMEM((D, FF), BF),
            pltpu.VMEM((D, FF), BF),
            pltpu.VMEM((FF, D), BF),
            pltpu.VMEM((2, CHUNKS[0][1], FF), F32),
            pltpu.VMEM((2, ROWS, D), BF),
            pltpu.VMEM((2, RELAYS * SLOT, D), BF),
            pltpu.VMEM((2, ROWS, D), BF),
            pltpu.VMEM((TOK, GL), BF),
            pltpu.VMEM((3, ROWS, FF), BF),
            pltpu.VMEM((ROWS, D), BF),
            pltpu.VMEM((ROWS, D), BF),
            pltpu.VMEM((ROWS, GL), BF),
            pltpu.VMEM((UNITS * MSGS, HALF, FF), BF),
            pltpu.VMEM((UNITS * MSGS, HALF, FF), BF),
            pltpu.VMEM((6, HALF, FF), F32),
            pltpu.VMEM((6, HALF, FF), BF),
            pltpu.VMEM((6, HALF, FF), BF),
            dma((7,)),
            dma((2,)),
            dma((2, RELAYS)),
            dma((2,)),
            dma((2, 3)),
            dma,
            dma,
            dma,
            dma((UNITS * MSGS,)),
            dma,
            dma((6,)),
        ],
        compiler_params=pltpu.CompilerParams(
            collective_id=0, has_side_effects=True, vmem_limit_bytes=52 * 2**20
        ),
    )(pltpu.with_memory_space_constraint(expert_ids.T, pltpu.HBM), pltpu.with_memory_space_constraint(gate_vals.T, pltpu.HBM), tokens, out_grad, w_gate, w_up, w_down)
    d_tokens, d_gates, d_gate, d_up, d_down = pl.pallas_call(
        settle,
        out_shape=shapes,
        in_specs=[hbm] * 5,
        out_specs=[hbm] * 5,
        scratch_shapes=[dma((5,))],
        compiler_params=pltpu.CompilerParams(vmem_limit_bytes=2**20),
    )(*outs)
    return d_tokens, d_gates.T, d_gate, d_up, d_down


def solution(mesh):
    in_specs = (
        P(("dp", "expert"), None),
        P(("dp", "expert"), None),
        P(("dp", "expert"), None),
        P(("dp", "expert"), None),
        P("expert", None, None),
        P("expert", None, None),
        P("expert", None, None),
    )
    out_specs = (
        P(("dp", "expert"), None),
        P(("dp", "expert"), None),
        P("expert", "dp", None),
        P("expert", "dp", None),
        P("expert", None, "dp"),
    )
    return jax.shard_map(body, mesh=mesh, in_specs=in_specs, out_specs=out_specs, check_vma=False)
```

```python
import functools

import jax
import jax.numpy as jnp
from jax import lax
from jax.experimental import pallas as pl
from jax.experimental.pallas import tpu as pltpu
from jax.sharding import PartitionSpec as P

MESH = pl.DeviceIdType.MESH
BF = jnp.bfloat16
F32 = jnp.float32

TOK = 160
TOP = 8
D = 2048
FF = 768
NE = 32
SLOT = 16
ROWS = NE * SLOT
GL = NE * SLOT
UNITS = 6
MSGS = 6
HALF = 128
FIRST = 14
RELAYS = NE - FIRST
WIDTH = D - 128
CHUNKS = ((0, 224), (224, 144), (368, 144))
LAST = CHUNKS[2][0] // SLOT


def coords():
    dp, ex = lax.axis_index("dp"), lax.axis_index("expert")
    return dp % 4, ex // 8, (dp // 4) * 4 + (ex // 2) % 4, ex % 2


def device(x, y, z, c):
    z = (z + 8) % 8
    return {"dp": (z // 4) * 4 + (x + 4) % 4, "expert": (((y + 4) % 4) * 4 + z % 4) * 2 + c}


def offset(j):
    q, r = j // 2, (j - FIRST) // 2
    plain = j < FIRST
    dy = jnp.where(plain, jnp.where(q < 4, q, 0), 1 + r % 3)
    kind = jnp.where(plain, jnp.where(q < 4, 0, q - 3), 1 + (r % 3 + r // 3) % 3)
    return dy, kind, j % 2


def z_shift(kind, core):
    return jnp.where(kind == 1, 1, 0) - jnp.where(kind == 2, 1, 0) + jnp.where(kind == 3, 2 - 4 * core, 0)


def target(j):
    x, y, z, c = coords()
    dy, kind, dc = offset(j)
    return device(x, y + dy, z + z_shift(kind, c), (c + dc) % 2)


def origin(j):
    x, y, z, c = coords()
    dy, kind, dc = offset(j)
    c0 = (c + dc) % 2
    return device(x, y - dy, z - z_shift(kind, c0), c0)


def target_expert(j):
    x, y, z, c = coords()
    dy, kind, dc = offset(j)
    return (((y + dy) % 4) * 4 + (z + z_shift(kind, c) + 8) % 4) * 2 + (c + dc) % 2


def turn(j, p, second):
    x, y, z, c = coords()
    dy, kind, dc = offset(j)
    if second == (p == 0):
        return device(x, y + dy, z, c)
    return device(x, y, z + z_shift(kind, c), (c + dc) % 2)


def peers():
    x, y, z, c = coords()
    for dz in (2, -2, 1, -1, 0):
        for dy in (2, 1, 3, 0):
            for dc in (0, 1):
                if (dz, dy, dc) != (0, 0, 0):
                    yield device(x, y + dy, z + dz, (c + dc) % 2)
    yield device(x + 1, y, z, c)
    yield device(x - 1, y, z, c)
    yield device(x, y, z + 4, c)


def block(j):
    return pl.ds(pl.multiple_of(j * SLOT, SLOT), SLOT)


def iota(shape, dim):
    return lax.broadcasted_iota(jnp.int32, shape, dim)


def kernel(
    ids_hbm, gate_hbm, tok_hbm, dy_hbm, wg_hbm, wu_hbm, wd_hbm,
    dtok_ref, dgate_ref, owg_ref, owu_ref, owd_ref,
    ids_ref, gate_ref, tok_ref, dy_ref, wg, wu, wd, pre, sent, relay, xs, taken, sel, gs, rt, back, dgs, rs_s, rs_r, own, z_s, z_r,
    w_sem, h_ss, h_rs, d_ss, d_rs, b_ss, b_rs, r_ss, r_rs, z_ss, z_rs,
):
    x, y, z, c = coords()
    me = lax.axis_index("expert")
    my_half = lax.axis_index("dp") // 4

    barrier = pltpu.get_barrier_semaphore()
    count = 0
    for peer in peers():
        pl.semaphore_signal(barrier, inc=1, device_id=peer, device_id_type=MESH)
        count += 1

    loads = [
        pltpu.make_async_copy(src, dst, w_sem.at[n])
        for n, (src, dst) in enumerate(
            ((ids_hbm, ids_ref), (gate_hbm, gate_ref), (tok_hbm, tok_ref), (dy_hbm, dy_ref), (wg_hbm.at[0], wg), (wu_hbm.at[0], wu), (wd_hbm.at[0], wd))
        )
    ]
    for load in loads:
        load.start()

    loads[0].wait()
    loads[1].wait()
    expert_of = iota((GL, TOK), 0) // SLOT
    member = jnp.zeros((GL, TOK), F32)
    value = jnp.zeros((GL, TOK), F32)
    for k in range(TOP):
        hit = ids_ref[k : k + 1, :] == expert_of
        member = jnp.where(hit, 1.0, member)
        value = jnp.where(hit, gate_ref[k : k + 1, :].astype(F32), value)
    earlier = (iota((TOK, TOK), 0) < iota((TOK, TOK), 1)).astype(F32).astype(BF)
    rank = jnp.dot(member.astype(BF), earlier, preferred_element_type=F32)
    slot_of = (iota((GL, TOK), 0) % SLOT).astype(F32)
    chosen = jnp.where(rank == slot_of, member, 0.0)
    picks = chosen.astype(BF), (chosen * value).astype(BF)
    taken[...] = picks[0]
    at_end = iota((NE, SLOT, 128), 1) == SLOT - 1

    def pack(p, ref):
        tail = jnp.dot(picks[p], ref[:, WIDTH:], preferred_element_type=F32).reshape(NE, SLOT, 128)
        for n in range(4):
            first, stop = n * 512, min(n * 512 + 512, WIDTH)
            rows = jnp.dot(picks[p], ref[:, first:stop], preferred_element_type=F32)
            for k in range(0, stop - first, 128):
                r = (first + k) // 128
                part = rows[:, k : k + 128].reshape(NE, SLOT, 128)
                part = jnp.where(at_end, tail[:, r : r + 1, :], part)
                sent[p, :, first + k : first + k + 128] = part.reshape(ROWS, 128).astype(BF)

    loads[2].wait()
    pack(0, tok_ref)

    pl.semaphore_wait(barrier, count)

    def arrival(p, j, src, to):
        return pltpu.make_async_remote_copy(
            src_ref=src,
            dst_ref=xs.at[p, block(j), 0 : WIDTH],
            send_sem=d_ss.at[p],
            recv_sem=d_rs.at[p, jnp.where(j < FIRST, 0, jnp.where(j < LAST, 1, 2))],
            device_id=to,
            device_id_type=MESH,
        )

    def direct(p, j):
        return arrival(p, j, sent.at[p, block(target_expert(j)), 0 : WIDTH], target(j))

    def hop(p, r):
        j = r + FIRST
        return pltpu.make_async_remote_copy(
            src_ref=sent.at[p, block(target_expert(j)), 0 : WIDTH],
            dst_ref=relay.at[p, block(r), 0 : WIDTH],
            send_sem=h_ss.at[p],
            recv_sem=h_rs.at[p, r],
            device_id=turn(j, p, False),
            device_id_type=MESH,
        )

    def onward(p, r):
        j = r + FIRST
        return arrival(p, j, relay.at[p, block(r), 0 : WIDTH], turn(j, p, True))

    @pl.loop(0, RELAYS)
    def _(r):
        hop(0, r).start()

    @pl.loop(1, FIRST)
    def _(j):
        direct(0, j).start()

    loads[3].wait()
    pack(1, dy_ref)

    @pl.loop(0, RELAYS)
    def _(r):
        hop(1, r).start()

    @pl.loop(1, FIRST)
    def _(j):
        direct(1, j).start()

    for p in range(2):
        xs[p, 0:SLOT, 0 : WIDTH] = sent[p, block(me), 0 : WIDTH]
    for load in loads[4:]:
        load.wait()

    @pl.loop(0, RELAYS)
    def _(r):
        for p in range(2):
            hop(p, r).wait_recv()
            onward(p, r).start()

    sel[...] = taken[...].astype(F32).T.astype(BF)

    lane = iota((1, SLOT, GL), 2)
    mine = lane == me * SLOT + iota((1, SLOT, GL), 1)

    def live(count):
        return iota((count, 1), 0) % SLOT < SLOT - 1

    def forward(rows, count):
        place = iota((1, SLOT, 128), 1)
        for p in range(2):
            tail = jnp.zeros((count // SLOT, SLOT, 128), F32)
            for r in range(SLOT - 1):
                part = xs[p, rows, r * 128 : (r + 1) * 128].astype(F32)
                part = part.reshape(count // SLOT, SLOT, 128)
                tail = jnp.where(place == r, part[:, SLOT - 1 : SLOT, :], tail)
            xs[p, rows, WIDTH:] = tail.reshape(count, 128).astype(BF)

        @pl.loop(0, FF // 256)
        def _(f):
            cols = pl.ds(pl.multiple_of(f * 256, 256), 256)
            gate_pre = jnp.dot(xs[0, rows, :], wg[:, cols], preferred_element_type=F32)
            up_pre = jnp.dot(xs[0, rows, :], wu[:, cols], preferred_element_type=F32)
            pre[0, 0:count, cols] = gate_pre
            pre[1, 0:count, cols] = up_pre
            hidden = gate_pre * jax.nn.sigmoid(gate_pre) * up_pre
            gs[0, rows, cols] = jnp.where(live(count), hidden, 0.0).astype(BF)

    def backward(rows, count):
        def part(f, total):
            cols = pl.ds(pl.multiple_of(f * 256, 256), 256)
            grad = lax.dot_general(
                xs[1, rows, :], wd[cols, :], (((1,), (1,)), ((), ())), preferred_element_type=F32
            )
            grad = jnp.where(live(count), grad, 0.0)
            gate_pre, up_pre = pre[0, 0:count, cols], pre[1, 0:count, cols]
            sig = jax.nn.sigmoid(gate_pre)
            gs[2, rows, cols] = (grad * gate_pre * sig).astype(BF)
            gs[1, rows, cols] = (grad * up_pre * sig * (1.0 + gate_pre * (1.0 - sig))).astype(BF)
            return total + jnp.sum(gs[0, rows, cols].astype(F32) * grad, axis=1, keepdims=True)

        total = lax.fori_loop(0, FF // 256, part, jnp.zeros((count, 1), F32))
        grads = total.astype(BF).astype(F32).reshape(count // SLOT, SLOT, 1)
        grads = jnp.sum(jnp.where(mine, grads, 0.0), axis=1, keepdims=True)
        grads = jnp.broadcast_to(grads, (count // SLOT, SLOT, GL)).reshape(count, GL)
        dgs[rows, :] = grads.astype(BF)

    def input_rows(rows, count):
        ends = iota((count, GL), 0) % SLOT == SLOT - 1

        @pl.loop(0, D // 512)
        def _(n):
            feats = pl.ds(pl.multiple_of(n * 512, 512), 512)
            contract = (((1,), (1,)), ((), ()))
            out = lax.dot_general(gs[1, rows, :], wg[feats, :], contract, preferred_element_type=F32)
            out = out + lax.dot_general(
                gs[2, rows, :], wu[feats, :], contract, preferred_element_type=F32
            )
            rt[rows, feats] = out.astype(BF)

        rt[rows, 0:GL] = jnp.where(ends, dgs[rows, :].astype(F32), rt[rows, 0:GL].astype(F32)).astype(BF)

    def give_back(j):
        return pltpu.make_async_remote_copy(
            src_ref=rt.at[block(j)],
            dst_ref=back.at[block(me)],
            send_sem=b_ss,
            recv_sem=b_rs,
            device_id=origin(j),
            device_id_type=MESH,
        )

    def return_blocks(start, count):
        @pl.loop(max(start // SLOT, 1), (start + count) // SLOT)
        def _(j):
            give_back(j).start()

    for n, (start, count) in enumerate(CHUNKS):
        first = max(start, SLOT)
        for p in range(2):
            here = xs.at[p, pl.ds(first, start + count - first), 0 : WIDTH]
            pltpu.make_async_copy(here, here, d_rs.at[p, n]).wait()
        if n == len(CHUNKS) - 1:
            return_blocks(0, start)
            back[block(me), :] = rt[0:SLOT, :]
        forward(pl.ds(start, count), count)
        if n < 2:
            backward(pl.ds(start, count), count)
        if n < 2:
            input_rows(pl.ds(start, count), count)

    def half_of(u):
        return jnp.where(u < 3, 1 - my_half, my_half)

    def tile(u, to_x, half):
        kind = u % 3
        start = (half_of(u) * 4 + (to_x + 4) % 4) * 256 + half * HALF
        left = xs[jnp.where(kind == 0, 1, 0), :, pl.ds(pl.multiple_of(start, HALF), HALF)]
        return lax.dot_general(
            left, gs[kind], (((0,), (0,)), ((), ())), preferred_element_type=F32
        )

    def message(u, m):
        step = 1 if m % 2 == 0 else -1
        return pltpu.make_async_remote_copy(
            src_ref=rs_s.at[u * MSGS + m],
            dst_ref=rs_r.at[u * MSGS + m],
            send_sem=r_ss,
            recv_sem=r_rs.at[u * MSGS + m],
            device_id=device(x + step, y, z, c),
            device_id_type=MESH,
        )

    def send(u, m, tile_value):
        rs_s[u * MSGS + m] = tile_value.astype(BF)
        message(u, m).start()

    def received(u, m):
        message(u, m).wait_recv()
        return rs_r[u * MSGS + m].astype(F32)

    def to_partner(n, half):
        return pltpu.make_async_remote_copy(
            src_ref=z_s.at[n * 2 + half],
            dst_ref=z_r.at[n * 2 + half],
            send_sem=z_ss,
            recv_sem=z_rs.at[n * 2 + half],
            device_id=device(x, y, z + 4, c),
            device_id_type=MESH,
        )

    def token_gradients():
        others = back.at[pl.ds(SLOT, ROWS - SLOT)]
        pltpu.make_async_copy(others, others, b_rs).wait()
        for n in range(D // 512):
            cols = pl.ds(n * 512, 512)
            dtok_ref[:, cols] = jnp.dot(sel[...], back[:, cols], preferred_element_type=F32).astype(BF)
        ends = iota((ROWS, GL), 0) % SLOT == SLOT - 1
        row = jnp.sum(jnp.where(ends, back[:, 0:GL].astype(F32), 0.0), axis=0, keepdims=True)
        picked = sel[...].astype(F32) * row
        at = iota((TOK, TOP), 1)
        named = ids_ref[...].T
        weights = gate_ref[...].astype(F32).T
        grads = jnp.zeros((TOK, TOP), F32)
        for k in range(TOP):
            hit = named[:, k : k + 1] == iota((TOK, GL), 1) // SLOT
            one = jnp.sum(jnp.where(hit, picked, 0.0), axis=1, keepdims=True)
            grads = jnp.where(at == k, one, grads)
        dgate_ref[...] = (grads / weights).T.astype(BF)

    def finish(n):
        ref = (owd_ref, owg_ref, owu_ref)[n]
        for half in range(2):
            to_partner(n, half).wait_recv()
            total = own[n * 2 + half] + z_r[n * 2 + half].astype(F32)
            if n == 0:
                ref[0, :, half * HALF : (half + 1) * HALF] = total.T.astype(BF)
            else:
                ref[0, half * HALF : (half + 1) * HALF, :] = total.astype(BF)

    @pl.loop(0, UNITS + 2)
    def _(v):
        @pl.when(v < UNITS)
        def _():
            u = v
            send(u, 0, tile(u, x + 2, 0))
            send(u, 1, tile(u, x + 2, 1))

        @pl.when(v == 1)
        def _():
            start = CHUNKS[2][0]
            input_rows(pl.ds(start, ROWS - start), ROWS - start)
            return_blocks(start, ROWS - start)

        @pl.when(v == UNITS)
        def _():
            token_gradients()
            finish(0)

        @pl.when(v == UNITS + 1)
        def _():
            finish(1)

        @pl.when((v >= 1) & (v < UNITS + 1))
        def _():
            u = v - 1
            send(u, 4, tile(u, x + 1, 0) + received(u, 0))
            send(u, 5, tile(u, x - 1, 1) + received(u, 1))

        @pl.when(v < UNITS)
        def _():
            u = v
            send(u, 2, tile(u, x + 1, 1))
            send(u, 3, tile(u, x - 1, 0))

        @pl.when(v == 0)
        def _():
            backward(pl.ds(CHUNKS[2][0], CHUNKS[2][1]), CHUNKS[2][1])

        @pl.when(v >= 2)
        def _():
            u = v - 2
            for half in range(2):
                total = tile(u, x, half) + received(u, 4 + half) + received(u, 3 - half)

                @pl.when(u < 3)
                def _():
                    z_s[u * 2 + half] = total.astype(BF)
                    to_partner(u, half).start()

                @pl.when(u >= 3)
                def _():
                    own[(u - 3) * 2 + half] = total

    finish(2)

    rest = pl.ds(SLOT, ROWS - SLOT)
    for ref, sem in (
        (xs.at[0, rest, 0 : WIDTH], d_ss.at[0]), (xs.at[1, rest, 0:WIDTH], d_ss.at[1]),
        (relay.at[0, :, 0 : WIDTH], h_ss.at[0]), (relay.at[1, :, 0:WIDTH], h_ss.at[1]), (rt.at[rest], b_ss), (rs_s, r_ss), (z_s, z_ss),
    ):
        pltpu.make_async_remote_copy(
            src_ref=ref, dst_ref=ref, send_sem=sem, recv_sem=sem,
            device_id=device(x + 1, y, z, c), device_id_type=MESH,
        ).wait_send()


def settle(*refs):
    ins, outs, sem = refs[:5], refs[5:10], refs[10]
    puts = [pltpu.make_async_copy(ins[i], outs[i], sem.at[i]) for i in range(5)]
    for put in puts:
        put.start()
    for put in puts:
        put.wait()


def body(tokens, out_grad, expert_ids, gate_vals, w_gate, w_up, w_down):
    vmem = pl.BlockSpec(memory_space=pltpu.VMEM)
    hbm = pl.BlockSpec(memory_space=pl.ANY)
    dma = pltpu.SemaphoreType.DMA
    shapes = (
        jax.ShapeDtypeStruct((TOK, D), BF),
        jax.ShapeDtypeStruct((TOP, TOK), BF),
        jax.ShapeDtypeStruct((1, 256, FF), BF),
        jax.ShapeDtypeStruct((1, 256, FF), BF),
        jax.ShapeDtypeStruct((1, FF, 256), BF),
    )
    outs = pl.pallas_call(
        kernel,
        out_shape=shapes,
        in_specs=[pl.BlockSpec(memory_space=pltpu.HBM)] * 2 + [hbm] * 5,
        out_specs=[vmem] * 5,
        scratch_shapes=[
            pltpu.VMEM((TOP, TOK), jnp.int32),
            pltpu.VMEM((TOP, TOK), BF),
            pltpu.VMEM((TOK, D), BF),
            pltpu.VMEM((TOK, D), BF),
            pltpu.VMEM((D, FF), BF),
            pltpu.VMEM((D, FF), BF),
            pltpu.VMEM((FF, D), BF),
            pltpu.VMEM((2, CHUNKS[0][1], FF), F32),
            pltpu.VMEM((2, ROWS, D), BF),
            pltpu.VMEM((2, RELAYS * SLOT, D), BF),
            pltpu.VMEM((2, ROWS, D), BF),
            pltpu.VMEM((GL, TOK), BF),
            pltpu.VMEM((TOK, GL), BF),
            pltpu.VMEM((3, ROWS, FF), BF),
            pltpu.VMEM((ROWS, D), BF),
            pltpu.VMEM((ROWS, D), BF),
            pltpu.VMEM((ROWS, GL), BF),
            pltpu.VMEM((UNITS * MSGS, HALF, FF), BF),
            pltpu.VMEM((UNITS * MSGS, HALF, FF), BF),
            pltpu.VMEM((6, HALF, FF), F32),
            pltpu.VMEM((6, HALF, FF), BF),
            pltpu.VMEM((6, HALF, FF), BF),
            dma((7,)),
            dma((2,)),
            dma((2, RELAYS)),
            dma((2,)),
            dma((2, 3)),
            dma,
            dma,
            dma,
            dma((UNITS * MSGS,)),
            dma,
            dma((6,)),
        ],
        compiler_params=pltpu.CompilerParams(
            collective_id=0, has_side_effects=True, vmem_limit_bytes=52 * 2**20
        ),
    )(pltpu.with_memory_space_constraint(expert_ids.T, pltpu.HBM), pltpu.with_memory_space_constraint(gate_vals.T, pltpu.HBM), tokens, out_grad, w_gate, w_up, w_down)
    d_tokens, d_gates, d_gate, d_up, d_down = pl.pallas_call(
        settle,
        out_shape=shapes,
        in_specs=[hbm] * 5,
        out_specs=[hbm] * 5,
        scratch_shapes=[dma((5,))],
        compiler_params=pltpu.CompilerParams(vmem_limit_bytes=2**20),
    )(*outs)
    return d_tokens, d_gates.T, d_gate, d_up, d_down


def solution(mesh):
    in_specs = (
        P(("dp", "expert"), None),
        P(("dp", "expert"), None),
        P(("dp", "expert"), None),
        P(("dp", "expert"), None),
        P("expert", None, None),
        P("expert", None, None),
        P("expert", None, None),
    )
    out_specs = (
        P(("dp", "expert"), None),
        P(("dp", "expert"), None),
        P("expert", "dp", None),
        P("expert", "dp", None),
        P("expert", None, "dp"),
    )
    return jax.shard_map(body, mesh=mesh, in_specs=in_specs, out_specs=out_specs, check_vma=False)
```

```python
import functools

import jax
import jax.numpy as jnp
from jax import lax
from jax.experimental import pallas as pl
from jax.experimental.pallas import tpu as pltpu
from jax.sharding import PartitionSpec as P

MESH = pl.DeviceIdType.MESH
BF = jnp.bfloat16
F32 = jnp.float32

TOK = 160
TOP = 8
D = 2048
FF = 768
NE = 32
SLOT = 16
ROWS = NE * SLOT
GL = NE * SLOT
UNITS = 6
MSGS = 6
HALF = 128
FIRST = 14
RELAYS = NE - FIRST
WIDTH = D - 128
CHUNKS = ((0, 224), (224, 144), (368, 144))
LAST = CHUNKS[2][0] // SLOT


def coords():
    dp, ex = lax.axis_index("dp"), lax.axis_index("expert")
    return dp % 4, ex // 8, (dp // 4) * 4 + (ex // 2) % 4, ex % 2


def device(x, y, z, c):
    z = (z + 8) % 8
    return {"dp": (z // 4) * 4 + (x + 4) % 4, "expert": (((y + 4) % 4) * 4 + z % 4) * 2 + c}


def offset(j):
    q, r = j // 2, (j - FIRST) // 2
    plain = j < FIRST
    dy = jnp.where(plain, jnp.where(q < 4, q, 0), 1 + r % 3)
    kind = jnp.where(plain, jnp.where(q < 4, 0, q - 3), 1 + (r % 3 + r // 3) % 3)
    return dy, kind, j % 2


def z_shift(kind, core):
    return jnp.where(kind == 1, 1, 0) - jnp.where(kind == 2, 1, 0) + jnp.where(kind == 3, 2 - 4 * core, 0)


def target(j):
    x, y, z, c = coords()
    dy, kind, dc = offset(j)
    return device(x, y + dy, z + z_shift(kind, c), (c + dc) % 2)


def origin(j):
    x, y, z, c = coords()
    dy, kind, dc = offset(j)
    c0 = (c + dc) % 2
    return device(x, y - dy, z - z_shift(kind, c0), c0)


def target_expert(j):
    x, y, z, c = coords()
    dy, kind, dc = offset(j)
    return (((y + dy) % 4) * 4 + (z + z_shift(kind, c) + 8) % 4) * 2 + (c + dc) % 2


def turn(j, p, second):
    x, y, z, c = coords()
    dy, kind, dc = offset(j)
    if second == (p == 0):
        return device(x, y + dy, z, c)
    return device(x, y, z + z_shift(kind, c), (c + dc) % 2)


def peers():
    x, y, z, c = coords()
    for dz in (2, -2, 1, -1, 0):
        for dy in (2, 1, 3, 0):
            for dc in (0, 1):
                if (dz, dy, dc) != (0, 0, 0):
                    yield device(x, y + dy, z + dz, (c + dc) % 2)
    yield device(x + 1, y, z, c)
    yield device(x - 1, y, z, c)
    yield device(x, y, z + 4, c)


def block(j):
    return pl.ds(pl.multiple_of(j * SLOT, SLOT), SLOT)


def iota(shape, dim):
    return lax.broadcasted_iota(jnp.int32, shape, dim)


def kernel(
    ids_hbm, gate_hbm, tok_hbm, dy_hbm, wg_hbm, wu_hbm, wd_hbm,
    dtok_ref, dgate_ref, owg_ref, owu_ref, owd_ref,
    ids_ref, gate_ref, tok_ref, dy_ref, wg, wu, wd, pre, sent, relay, xs, taken, sel, gs, rt, back, dgs, rs_s, rs_r, own, z_s, z_r,
    w_sem, h_ss, h_rs, d_ss, d_rs, b_ss, b_rs, r_ss, r_rs, z_ss, z_rs,
):
    x, y, z, c = coords()
    me = lax.axis_index("expert")
    my_half = lax.axis_index("dp") // 4

    barrier = pltpu.get_barrier_semaphore()
    count = 0
    for peer in peers():
        pl.semaphore_signal(barrier, inc=1, device_id=peer, device_id_type=MESH)
        count += 1

    loads = [
        pltpu.make_async_copy(src, dst, w_sem.at[n])
        for n, (src, dst) in enumerate(
            ((ids_hbm, ids_ref), (gate_hbm, gate_ref), (tok_hbm, tok_ref), (dy_hbm, dy_ref), (wg_hbm.at[0], wg), (wu_hbm.at[0], wu), (wd_hbm.at[0], wd))
        )
    ]
    for load in loads:
        load.start()

    loads[0].wait()
    loads[1].wait()
    expert_of = iota((GL, TOK), 0) // SLOT
    member = jnp.zeros((GL, TOK), F32)
    value = jnp.zeros((GL, TOK), F32)
    for k in range(TOP):
        hit = ids_ref[k : k + 1, :] == expert_of
        member = jnp.where(hit, 1.0, member)
        value = jnp.where(hit, gate_ref[k : k + 1, :].astype(F32), value)
    earlier = (iota((TOK, TOK), 0) < iota((TOK, TOK), 1)).astype(F32).astype(BF)
    rank = jnp.dot(member.astype(BF), earlier, preferred_element_type=F32)
    slot_of = (iota((GL, TOK), 0) % SLOT).astype(F32)
    chosen = jnp.where(rank == slot_of, member, 0.0)
    picks = chosen.astype(BF), (chosen * value).astype(BF)
    taken[...] = picks[0]
    at_end = iota((NE, SLOT, 128), 1) == SLOT - 1

    def pack(p, ref):
        tail = jnp.dot(picks[p], ref[:, WIDTH:], preferred_element_type=F32).reshape(NE, SLOT, 128)
        for n in range(4):
            first, stop = n * 512, min(n * 512 + 512, WIDTH)
            rows = jnp.dot(picks[p], ref[:, first:stop], preferred_element_type=F32)
            for k in range(0, stop - first, 128):
                r = (first + k) // 128
                part = rows[:, k : k + 128].reshape(NE, SLOT, 128)
                part = jnp.where(at_end, tail[:, r : r + 1, :], part)
                sent[p, :, first + k : first + k + 128] = part.reshape(ROWS, 128).astype(BF)

    loads[2].wait()
    pack(0, tok_ref)

    pl.semaphore_wait(barrier, count)

    def arrival(p, j, src, to):
        return pltpu.make_async_remote_copy(
            src_ref=src,
            dst_ref=xs.at[p, block(j), 0 : WIDTH],
            send_sem=d_ss.at[p],
            recv_sem=d_rs.at[p, jnp.where(j < FIRST, 0, jnp.where(j < LAST, 1, 2))],
            device_id=to,
            device_id_type=MESH,
        )

    def direct(p, j):
        return arrival(p, j, sent.at[p, block(target_expert(j)), 0 : WIDTH], target(j))

    def hop(p, r):
        j = r + FIRST
        return pltpu.make_async_remote_copy(
            src_ref=sent.at[p, block(target_expert(j)), 0 : WIDTH],
            dst_ref=relay.at[p, block(r), 0 : WIDTH],
            send_sem=h_ss.at[p],
            recv_sem=h_rs.at[p, r // 2],
            device_id=turn(j, p, False),
            device_id_type=MESH,
        )

    def onward(p, r):
        j = r + FIRST
        return arrival(p, j, relay.at[p, block(r), 0 : WIDTH], turn(j, p, True))

    @pl.loop(0, RELAYS)
    def _(r):
        hop(0, r).start()

    @pl.loop(1, FIRST)
    def _(j):
        direct(0, j).start()

    loads[3].wait()
    pack(1, dy_ref)

    @pl.loop(0, RELAYS)
    def _(r):
        hop(1, r).start()

    @pl.loop(1, FIRST)
    def _(j):
        direct(1, j).start()

    for p in range(2):
        xs[p, 0:SLOT, 0 : WIDTH] = sent[p, block(me), 0 : WIDTH]
    for load in loads[4:]:
        load.wait()

    @pl.loop(0, RELAYS // 2)
    def _(q):
        for p in range(2):
            both = relay.at[p, pl.ds(pl.multiple_of(q * 2 * SLOT, 2 * SLOT), 2 * SLOT), 0:WIDTH]
            pltpu.make_async_copy(both, both, h_rs.at[p, q]).wait()
            onward(p, q * 2).start()
            onward(p, q * 2 + 1).start()

    sel[...] = taken[...].astype(F32).T.astype(BF)

    lane = iota((1, SLOT, GL), 2)
    mine = lane == me * SLOT + iota((1, SLOT, GL), 1)

    def live(count):
        return iota((count, 1), 0) % SLOT < SLOT - 1

    def forward(rows, count):
        place = iota((1, SLOT, 128), 1)
        for p in range(2):
            tail = jnp.zeros((count // SLOT, SLOT, 128), F32)
            for r in range(SLOT - 1):
                part = xs[p, rows, r * 128 : (r + 1) * 128].astype(F32)
                part = part.reshape(count // SLOT, SLOT, 128)
                tail = jnp.where(place == r, part[:, SLOT - 1 : SLOT, :], tail)
            xs[p, rows, WIDTH:] = tail.reshape(count, 128).astype(BF)

        @pl.loop(0, FF // 256)
        def _(f):
            cols = pl.ds(pl.multiple_of(f * 256, 256), 256)
            gate_pre = jnp.dot(xs[0, rows, :], wg[:, cols], preferred_element_type=F32)
            up_pre = jnp.dot(xs[0, rows, :], wu[:, cols], preferred_element_type=F32)
            pre[0, 0:count, cols] = gate_pre
            pre[1, 0:count, cols] = up_pre
            hidden = gate_pre * jax.nn.sigmoid(gate_pre) * up_pre
            gs[0, rows, cols] = jnp.where(live(count), hidden, 0.0).astype(BF)

    def backward(rows, count):
        def part(f, total):
            cols = pl.ds(pl.multiple_of(f * 256, 256), 256)
            grad = lax.dot_general(
                xs[1, rows, :], wd[cols, :], (((1,), (1,)), ((), ())), preferred_element_type=F32
            )
            grad = jnp.where(live(count), grad, 0.0)
            gate_pre, up_pre = pre[0, 0:count, cols], pre[1, 0:count, cols]
            sig = jax.nn.sigmoid(gate_pre)
            gs[2, rows, cols] = (grad * gate_pre * sig).astype(BF)
            gs[1, rows, cols] = (grad * up_pre * sig * (1.0 + gate_pre * (1.0 - sig))).astype(BF)
            return total + jnp.sum(gs[0, rows, cols].astype(F32) * grad, axis=1, keepdims=True)

        total = lax.fori_loop(0, FF // 256, part, jnp.zeros((count, 1), F32))
        grads = total.astype(BF).astype(F32).reshape(count // SLOT, SLOT, 1)
        grads = jnp.sum(jnp.where(mine, grads, 0.0), axis=1, keepdims=True)
        grads = jnp.broadcast_to(grads, (count // SLOT, SLOT, GL)).reshape(count, GL)
        dgs[rows, :] = grads.astype(BF)

    def input_rows(rows, count):
        ends = iota((count, GL), 0) % SLOT == SLOT - 1

        @pl.loop(0, D // 512)
        def _(n):
            feats = pl.ds(pl.multiple_of(n * 512, 512), 512)
            contract = (((1,), (1,)), ((), ()))
            out = lax.dot_general(gs[1, rows, :], wg[feats, :], contract, preferred_element_type=F32)
            out = out + lax.dot_general(
                gs[2, rows, :], wu[feats, :], contract, preferred_element_type=F32
            )
            rt[rows, feats] = out.astype(BF)

        rt[rows, 0:GL] = jnp.where(ends, dgs[rows, :].astype(F32), rt[rows, 0:GL].astype(F32)).astype(BF)

    def give_back(j):
        return pltpu.make_async_remote_copy(
            src_ref=rt.at[block(j)],
            dst_ref=back.at[block(me)],
            send_sem=b_ss,
            recv_sem=b_rs,
            device_id=origin(j),
            device_id_type=MESH,
        )

    def return_blocks(start, count):
        @pl.loop(max(start // SLOT, 1), (start + count) // SLOT)
        def _(j):
            give_back(j).start()

    for n, (start, count) in enumerate(CHUNKS):
        first = max(start, SLOT)
        for p in range(2):
            here = xs.at[p, pl.ds(first, start + count - first), 0 : WIDTH]
            pltpu.make_async_copy(here, here, d_rs.at[p, n]).wait()
        if n == len(CHUNKS) - 1:
            return_blocks(0, start)
            back[block(me), :] = rt[0:SLOT, :]
        forward(pl.ds(start, count), count)
        if n < 2:
            backward(pl.ds(start, count), count)
        if n < 2:
            input_rows(pl.ds(start, count), count)

    def half_of(u):
        return jnp.where(u < 3, 1 - my_half, my_half)

    def tile(u, to_x, half):
        kind = u % 3
        start = (half_of(u) * 4 + (to_x + 4) % 4) * 256 + half * HALF
        left = xs[jnp.where(kind == 0, 1, 0), :, pl.ds(pl.multiple_of(start, HALF), HALF)]
        return lax.dot_general(
            left, gs[kind], (((0,), (0,)), ((), ())), preferred_element_type=F32
        )

    def message(u, m):
        step = 1 if m % 2 == 0 else -1
        return pltpu.make_async_remote_copy(
            src_ref=rs_s.at[u * MSGS + m],
            dst_ref=rs_r.at[u * MSGS + m],
            send_sem=r_ss,
            recv_sem=r_rs.at[u * 3 + min(m, 2)],
            device_id=device(x + step, y, z, c),
            device_id_type=MESH,
        )

    def send(u, m, tile_value):
        rs_s[u * MSGS + m] = tile_value.astype(BF)
        message(u, m).start()

    def received(u, m):
        message(u, m).wait_recv()
        return rs_r[u * MSGS + m].astype(F32)

    def to_partner(n, half):
        return pltpu.make_async_remote_copy(
            src_ref=z_s.at[n * 2 + half],
            dst_ref=z_r.at[n * 2 + half],
            send_sem=z_ss,
            recv_sem=z_rs.at[n * 2 + half],
            device_id=device(x, y, z + 4, c),
            device_id_type=MESH,
        )

    def token_gradients():
        others = back.at[pl.ds(SLOT, ROWS - SLOT)]
        pltpu.make_async_copy(others, others, b_rs).wait()
        for n in range(D // 512):
            cols = pl.ds(n * 512, 512)
            dtok_ref[:, cols] = jnp.dot(sel[...], back[:, cols], preferred_element_type=F32).astype(BF)
        ends = iota((ROWS, GL), 0) % SLOT == SLOT - 1
        row = jnp.sum(jnp.where(ends, back[:, 0:GL].astype(F32), 0.0), axis=0, keepdims=True)
        picked = sel[...].astype(F32) * row
        at = iota((TOK, TOP), 1)
        named = ids_ref[...].T
        weights = gate_ref[...].astype(F32).T
        grads = jnp.zeros((TOK, TOP), F32)
        for k in range(TOP):
            hit = named[:, k : k + 1] == iota((TOK, GL), 1) // SLOT
            one = jnp.sum(jnp.where(hit, picked, 0.0), axis=1, keepdims=True)
            grads = jnp.where(at == k, one, grads)
        dgate_ref[...] = (grads / weights).T.astype(BF)

    def finish(n):
        ref = (owd_ref, owg_ref, owu_ref)[n]
        for half in range(2):
            to_partner(n, half).wait_recv()
            total = own[n * 2 + half] + z_r[n * 2 + half].astype(F32)
            if n == 0:
                ref[0, :, half * HALF : (half + 1) * HALF] = total.T.astype(BF)
            else:
                ref[0, half * HALF : (half + 1) * HALF, :] = total.astype(BF)

    @pl.loop(0, UNITS + 2)
    def _(v):
        @pl.when(v < UNITS)
        def _():
            u = v
            send(u, 0, tile(u, x + 2, 0))
            send(u, 1, tile(u, x + 2, 1))

        @pl.when(v == 1)
        def _():
            start = CHUNKS[2][0]
            input_rows(pl.ds(start, ROWS - start), ROWS - start)
            return_blocks(start, ROWS - start)

        @pl.when(v == UNITS)
        def _():
            token_gradients()
            finish(0)

        @pl.when(v == UNITS + 1)
        def _():
            finish(1)

        @pl.when((v >= 1) & (v < UNITS + 1))
        def _():
            u = v - 1
            send(u, 4, tile(u, x + 1, 0) + received(u, 0))
            send(u, 5, tile(u, x - 1, 1) + received(u, 1))

        @pl.when(v < UNITS)
        def _():
            u = v
            send(u, 2, tile(u, x + 1, 1))
            send(u, 3, tile(u, x - 1, 0))

        @pl.when(v == 0)
        def _():
            backward(pl.ds(CHUNKS[2][0], CHUNKS[2][1]), CHUNKS[2][1])

        @pl.when(v >= 2)
        def _():
            u = v - 2
            four = rs_r.at[pl.ds(u * MSGS + 2, 4)]
            pltpu.make_async_copy(four, four, r_rs.at[u * 3 + 2]).wait()
            for half in range(2):
                got = rs_r[u * MSGS + 4 + half].astype(F32) + rs_r[u * MSGS + 3 - half].astype(F32)
                total = tile(u, x, half) + got

                @pl.when(u < 3)
                def _():
                    z_s[u * 2 + half] = total.astype(BF)
                    to_partner(u, half).start()

                @pl.when(u >= 3)
                def _():
                    own[(u - 3) * 2 + half] = total

    finish(2)

    rest = pl.ds(SLOT, ROWS - SLOT)
    for ref, sem in (
        (xs.at[0, rest, 0 : WIDTH], d_ss.at[0]), (xs.at[1, rest, 0:WIDTH], d_ss.at[1]),
        (relay.at[0, :, 0 : WIDTH], h_ss.at[0]), (relay.at[1, :, 0:WIDTH], h_ss.at[1]), (rt.at[rest], b_ss), (rs_s, r_ss), (z_s, z_ss),
    ):
        pltpu.make_async_remote_copy(
            src_ref=ref, dst_ref=ref, send_sem=sem, recv_sem=sem,
            device_id=device(x + 1, y, z, c), device_id_type=MESH,
        ).wait_send()


def settle(*refs):
    ins, outs, sem = refs[:5], refs[5:10], refs[10]
    puts = [pltpu.make_async_copy(ins[i], outs[i], sem.at[i]) for i in range(5)]
    for put in puts:
        put.start()
    for put in puts:
        put.wait()


def body(tokens, out_grad, expert_ids, gate_vals, w_gate, w_up, w_down):
    vmem = pl.BlockSpec(memory_space=pltpu.VMEM)
    hbm = pl.BlockSpec(memory_space=pl.ANY)
    dma = pltpu.SemaphoreType.DMA
    shapes = (
        jax.ShapeDtypeStruct((TOK, D), BF),
        jax.ShapeDtypeStruct((TOP, TOK), BF),
        jax.ShapeDtypeStruct((1, 256, FF), BF),
        jax.ShapeDtypeStruct((1, 256, FF), BF),
        jax.ShapeDtypeStruct((1, FF, 256), BF),
    )
    outs = pl.pallas_call(
        kernel,
        out_shape=shapes,
        in_specs=[pl.BlockSpec(memory_space=pltpu.HBM)] * 2 + [hbm] * 5,
        out_specs=[vmem] * 5,
        scratch_shapes=[
            pltpu.VMEM((TOP, TOK), jnp.int32),
            pltpu.VMEM((TOP, TOK), BF),
            pltpu.VMEM((TOK, D), BF),
            pltpu.VMEM((TOK, D), BF),
            pltpu.VMEM((D, FF), BF),
            pltpu.VMEM((D, FF), BF),
            pltpu.VMEM((FF, D), BF),
            pltpu.VMEM((2, CHUNKS[0][1], FF), F32),
            pltpu.VMEM((2, ROWS, D), BF),
            pltpu.VMEM((2, RELAYS * SLOT, D), BF),
            pltpu.VMEM((2, ROWS, D), BF),
            pltpu.VMEM((GL, TOK), BF),
            pltpu.VMEM((TOK, GL), BF),
            pltpu.VMEM((3, ROWS, FF), BF),
            pltpu.VMEM((ROWS, D), BF),
            pltpu.VMEM((ROWS, D), BF),
            pltpu.VMEM((ROWS, GL), BF),
            pltpu.VMEM((UNITS * MSGS, HALF, FF), BF),
            pltpu.VMEM((UNITS * MSGS, HALF, FF), BF),
            pltpu.VMEM((6, HALF, FF), F32),
            pltpu.VMEM((6, HALF, FF), BF),
            pltpu.VMEM((6, HALF, FF), BF),
            dma((7,)),
            dma((2,)),
            dma((2, RELAYS // 2)),
            dma((2,)),
            dma((2, 3)),
            dma,
            dma,
            dma,
            dma((UNITS * 3,)),
            dma,
            dma((6,)),
        ],
        compiler_params=pltpu.CompilerParams(
            collective_id=0, has_side_effects=True, vmem_limit_bytes=52 * 2**20
        ),
    )(pltpu.with_memory_space_constraint(expert_ids.T, pltpu.HBM), pltpu.with_memory_space_constraint(gate_vals.T, pltpu.HBM), tokens, out_grad, w_gate, w_up, w_down)
    d_tokens, d_gates, d_gate, d_up, d_down = pl.pallas_call(
        settle,
        out_shape=shapes,
        in_specs=[hbm] * 5,
        out_specs=[hbm] * 5,
        scratch_shapes=[dma((5,))],
        compiler_params=pltpu.CompilerParams(vmem_limit_bytes=2**20),
    )(*outs)
    return d_tokens, d_gates.T, d_gate, d_up, d_down


def solution(mesh):
    in_specs = (
        P(("dp", "expert"), None),
        P(("dp", "expert"), None),
        P(("dp", "expert"), None),
        P(("dp", "expert"), None),
        P("expert", None, None),
        P("expert", None, None),
        P("expert", None, None),
    )
    out_specs = (
        P(("dp", "expert"), None),
        P(("dp", "expert"), None),
        P("expert", "dp", None),
        P("expert", "dp", None),
        P("expert", None, "dp"),
    )
    return jax.shard_map(body, mesh=mesh, in_specs=in_specs, out_specs=out_specs, check_vma=False)
```
